32 devices in a mesh: table: 4 (over y, core), cand: 8 (over z, x).
Axes of the slice: x: 2, y: 2, z: 4, core: 2. Of those that a mesh axis runs over, the one named last changes fastest.
Arguments:
- user_feats: bfloat16 [16, 4096], P('cand'), may hold values from -6 to 6
- tower_weight: bfloat16 [4096, 4096], P(None, 'table'), may hold values from -0.09375 to 0.09375
- tower_bias: float32 [4096], P('table'), may hold values from -3 to 3
- user_proj: bfloat16 [4096, 1024], P('table'), may hold values from -0.09375 to 0.09375
- item_ids: int32 [8, 16, 512], P('table', None, 'cand'), may hold values from 0 to 65535, as said below
- tables: bfloat16 [8, 65536, 128], P('table', 'cand'), may hold values from -6 to 6
- cross_weight: bfloat16 [1024, 1024], replicated, may hold values from -0.1875 to 0.1875
- cross_bias: float32 [1024], replicated, may hold values from -1 to 1
- mlp_first: bfloat16 [1024, 4096], P(None, 'table'), may hold values from -0.1875 to 0.1875
- first_bias: float32 [4096], P('table'), may hold values from -3 to 3
- mlp_second: bfloat16 [4096, 1024], P('table'), may hold values from -0.09375 to 0.09375
- second_bias: float32 [1024], replicated, may hold values from -3 to 3
- task_weight: bfloat16 [1024, 8], replicated, may hold values from -0.1875 to 0.1875
- task_bias: float32 [8], replicated, may hold values from -4 to 4
Outputs:
- logits: float32 [8, 16, 512], P(None, 'table', 'cand')
The draws below stay inside these ranges and needn't reach their ends.
Inputs may be any that keep to these rules, and one draw needn't show every extreme that they name: `item_ids`: rows k * 8192 to (k + 1) * 8192 - 1 of a table lie on index k of cand. For each table and each index of cand, that device's candidates of all requests name at most 256 ids lying on any one index of cand, and exactly 256 for one of them.
All inputs are finite; a program needn't handle non-finite values.
Results may differ from the reference program's by a relative error of at most 0.014.
Values may be sent and summed in bfloat16 or wider, within the bound.
A program may use at most 128 MiB of HBM per device.

```python
import jax
import jax.numpy as jnp
from jax import lax

DU = 4096
E = 128
HID = 4096
TOP = 1024
TASKS = 8
ROWS_DEV = 8192
CAND_DEV = 64
REQUESTS = 16
CANDS = 512
NTAB = 8
VOCAB = 65536
D0 = 1024
CAP = 256
N_CAND = 8


def draw_item_ids(key, part):
    row_count = REQUESTS * CAND_DEV
    key_hot, key_rows, key_perm = jax.random.split(jax.random.fold_in(key, 11), 3)
    hottest = jax.random.randint(key_hot, (NTAB, N_CAND), 0, N_CAND)
    hottest = hottest.at[0, 0].set(N_CAND - 1)
    places = jnp.arange(row_count)[None, None, :]
    spread = (places - CAP) % (N_CAND - 1)
    spread = spread + (spread >= hottest[:, :, None]).astype(jnp.int32)
    owners = jnp.where(places < CAP, hottest[:, :, None], spread)
    local_rows = jax.random.randint(key_rows, (NTAB, N_CAND, row_count), 0, ROWS_DEV)
    local_rows = jnp.where(places == 0, ROWS_DEV - 1, local_rows)
    joined = (owners * ROWS_DEV + local_rows).reshape(NTAB * N_CAND, row_count)
    perm_keys = jax.random.split(key_perm, NTAB * N_CAND)

    def shuffle(one_key, values):
        return jax.random.permutation(one_key, values)
    mixed = jax.vmap(shuffle)(perm_keys, joined)
    mixed = mixed.reshape(NTAB, N_CAND, REQUESTS, CAND_DEV)
    mixed = jnp.transpose(mixed, (0, 2, 1, 3)).reshape(NTAB, REQUESTS, CANDS)
    return mixed.astype(jnp.int32)


def block_levels(rng, shape, pieces, least, top_value):
    def one(position, shards_of):
        draws = jax.random.uniform(jax.random.fold_in(jax.random.fold_in(rng, 6), position), (shards_of,), jnp.float32, least / len(pieces), top_value / len(pieces))
        return jnp.repeat(jnp.exp(draws), shape[position] // shards_of).reshape((-1,) + (1,) * (len(shape) - position - 1))

    factor_of = one(*pieces[0])
    for cut in pieces[1:]:
        factor_of = factor_of * one(*cut)
    return factor_of


def bell_draw(own_key, extent, scale, bound, cuts=(), held_as=jnp.bfloat16):
    values = scale * jax.random.normal(own_key, extent, jnp.float32)
    if cuts:
        values = values * block_levels(own_key, extent, cuts, -0.22, 0.18)
    return jnp.clip(values, -bound, bound).astype(held_as)


def setup_inputs(seed: int = 0) -> dict:
    streams_of = jax.random.split(jax.random.key(seed), 15)
    return {
        "user_feats": bell_draw(streams_of[0], (REQUESTS, DU), 1.0, 6.0, ((0, 8),)),
        "tower_weight": bell_draw(streams_of[1], (DU, DU), DU ** -0.5, 0.09375, ((1, 4),)),
        "tower_bias": bell_draw(streams_of[2], (DU,), 0.5, 3.0, ((0, 4),), jnp.float32),
        "user_proj": bell_draw(streams_of[3], (DU, D0), DU ** -0.5, 0.09375, ((0, 4),)),
        "item_ids": draw_item_ids(jax.random.fold_in(streams_of[14], 71), 0),
        "tables": bell_draw(streams_of[5], (NTAB, VOCAB, E), 1.0, 6.0, ((0, 4), (1, 8))),
        "cross_weight": bell_draw(streams_of[6], (D0, D0), D0 ** -0.5, 0.1875),
        "cross_bias": jnp.clip(jax.random.uniform(streams_of[7], (D0,), jnp.float32, -1.0, 1.0), -1.0, 1.0),
        "mlp_first": bell_draw(streams_of[8], (D0, HID), D0 ** -0.5, 0.1875, ((1, 4),)),
        "first_bias": bell_draw(streams_of[9], (HID,), 0.5, 3.0, ((0, 4),), jnp.float32),
        "mlp_second": bell_draw(streams_of[10], (HID, TOP), HID ** -0.5, 0.09375, ((0, 4),)),
        "second_bias": bell_draw(streams_of[11], (TOP,), 0.5, 3.0, (), jnp.float32),
        "task_weight": bell_draw(streams_of[12], (TOP, TASKS), TOP ** -0.5, 0.1875),
        "task_bias": bell_draw(streams_of[13], (TASKS,), 1.0, 4.0, (), jnp.float32),
    }


def reference(user_feats, tower_weight, tower_bias, user_proj, item_ids, tables, cross_weight, cross_bias, mlp_first, first_bias, mlp_second, second_bias, task_weight, task_bias):
    tower = jax.nn.relu(jnp.dot(user_feats, tower_weight, preferred_element_type=jnp.float32) + tower_bias).astype(jnp.bfloat16)
    projected = jnp.dot(tower, user_proj, preferred_element_type=jnp.float32).astype(jnp.bfloat16)

    def pick_rows(table_rows, wanted):
        return jnp.take(table_rows, wanted, axis=0)

    def one_request(packed):
        request_ids, request_proj = packed
        fetched = jax.vmap(pick_rows)(tables, request_ids)
        joined = jnp.transpose(fetched, (1, 0, 2)).reshape(CANDS, NTAB * E)
        base = (joined.astype(jnp.float32) + request_proj.astype(jnp.float32)[None, :]).astype(jnp.bfloat16)
        product = jnp.dot(base, cross_weight, preferred_element_type=jnp.float32)
        base_wide = base.astype(jnp.float32)
        crossed = (base_wide * (product + cross_bias) + base_wide).astype(jnp.bfloat16)
        hidden = jax.nn.relu(jnp.dot(crossed, mlp_first, preferred_element_type=jnp.float32) + first_bias).astype(jnp.bfloat16)
        top = jax.nn.relu(jnp.dot(hidden, mlp_second, preferred_element_type=jnp.float32) + second_bias).astype(jnp.bfloat16)
        scores = jnp.dot(top, task_weight, preferred_element_type=jnp.float32) + task_bias
        return jnp.transpose(scores, (1, 0))

    result = lax.map(one_request, (jnp.transpose(item_ids, (1, 0, 2)), projected))
    return jnp.transpose(result, (1, 0, 2))
```

```python
import functools
import math

import jax
import jax.numpy as jnp
from jax import lax
from jax.experimental import pallas as pl
from jax.experimental.pallas import tpu as pltpu
from jax.sharding import PartitionSpec as P

MESH = pl.DeviceIdType.MESH
VMEM_SPEC = pl.BlockSpec(memory_space=pltpu.VMEM)
SMEM_SPEC = pl.BlockSpec(memory_space=pltpu.SMEM)
ANY_SPEC = pl.BlockSpec(memory_space=pl.ANY)
CORES = 2
LANES = 128
LIMIT = 62 << 20


def push(src, dst, send, recv, axis, peer):
    return pltpu.make_async_remote_copy(
        src_ref=src,
        dst_ref=dst,
        send_sem=send,
        recv_sem=recv,
        device_id={axis: peer},
        device_id_type=MESH,
    )


def widen(src, dst, rows):
    size = math.gcd(rows, 256)

    def body(i, carry):
        at = pl.multiple_of(i * size, size)
        dst[pl.ds(at, size), :] = src[pl.ds(at, size), :].astype(jnp.float32)
        return carry

    lax.fori_loop(0, rows // size, body, 0)


def whole_kernel(
    n,
    n_table,
    cap,
    owner,
    local,
    feats,
    tab,
    tower_w,
    tower_b,
    proj_w,
    first,
    second,
    bias,
    cross_w,
    cross_b,
    second_b,
    task_w,
    task_b,
    out,
    ids_o,
    ids_v,
    ids_s,
    spots,
    columns,
    feats_v,
    feats_f,
    tab_v,
    wide,
    found,
    blocks,
    summed,
    partial,
    parts,
    w_held,
    p_held,
    cross_v,
    first_v,
    second_v,
    biases,
    base,
    crossed,
    sent,
    got,
    load,
    id_send,
    id_recv,
    spot_send,
    spot_recv,
    row_send,
    row_recv,
    mate_send,
    mate_recv,
    level_send,
    level_recv,
    w_send,
    w_recv,
    part_send,
    part_recv,
    top_send,
    top_recv,
):
    me = lax.axis_index("cand")
    place = lax.axis_index("table")
    core = lax.rem(place, CORES)
    level = place // CORES
    levels = n_table // CORES
    mate = place + 1 - 2 * core
    tab_dev, steps, lanes = owner.shape
    per = tab_dev * cap
    lines = per // LANES
    embed = wide.shape[1]
    row_all = columns.shape[0]
    rows, width = base.shape
    tables_all = n_table * tab_dev
    tasks, requests, cand_dev = out.shape

    tab_copy = pltpu.make_async_copy(tab, tab_v.at[pl.ds(0, tab.shape[0]), :], load.at[0])
    w_copy = pltpu.make_async_copy(tower_w, w_held, load.at[1])
    p_copy = pltpu.make_async_copy(proj_w, p_held, load.at[2])
    held = [
        pltpu.make_async_copy(src, dst, load.at[5 + i])
        for i, (src, dst) in enumerate(
            ((cross_w, cross_v), (first, first_v.at[0]), (second, second_v.at[0]))
        )
    ]
    tab_copy.start()
    barrier = pltpu.get_barrier_semaphore()
    for d in range(1, n):
        pl.semaphore_signal(
            barrier, inc=1, device_id={"cand": lax.rem(me + d, n)}, device_id_type=MESH
        )
    for d in range(1, n_table):
        pl.semaphore_signal(
            barrier,
            inc=1,
            device_id={"table": lax.rem(place + d, n_table)},
            device_id_type=MESH,
        )

    owners = lax.broadcasted_iota(jnp.int32, (n, lanes), 0)
    sender = lax.broadcasted_iota(jnp.int32, (lanes, 2 * lanes), 0)
    reader = lax.broadcasted_iota(jnp.int32, (lanes, 2 * lanes), 1)
    counting = jnp.where((sender < reader) | (reader >= lanes), 1.0, 0.0).astype(jnp.bfloat16)
    slots = lax.broadcasted_iota(jnp.int32, (cap, lanes), 0).astype(jnp.float32)
    share = steps // n_table
    for t in range(tab_dev):
        hots = []
        for j in range(steps):
            hots.append(jnp.where(owner[t, j : j + 1, :] == owners, 1.0, 0.0))
        counts = jnp.dot(
            jnp.concatenate(hots, axis=0).astype(jnp.bfloat16),
            counting,
            preferred_element_type=jnp.float32,
        )
        before = jnp.zeros((n, lanes), jnp.float32)
        total = jnp.zeros((2 * n, cap), jnp.float32)
        for j in range(steps):
            hot = hots[j]
            mine = counts[j * n : (j + 1) * n, :]
            spot = jnp.sum(hot * (mine[:, 0:lanes] + before), axis=0, keepdims=True)
            before = before + mine[:, lanes:]
            spots[place, j // share, t, j % share : j % share + 1, :] = (
                spot + (owner[t, j : j + 1, :] * cap).astype(jnp.float32)
            )
            row = local[t, j : j + 1, :]
            low = (row & (LANES - 1)).astype(jnp.float32)
            high = (row // LANES).astype(jnp.float32)
            digits = jnp.concatenate([hot * low, hot * high], axis=0).astype(jnp.bfloat16)
            at = jnp.where(slots == spot, 1.0, 0.0).astype(jnp.bfloat16)
            total = total + lax.dot_general(
                digits, at, (((1,), (1,)), ((), ())), preferred_element_type=jnp.float32
            )
        offset = t * (tab.shape[0] // tab_dev)
        listed = (total[0:n] + total[n:] * float(LANES)).astype(jnp.int32) + offset
        listed = jnp.minimum(jnp.maximum(listed, 0), tab.shape[0] - 1)
        for o in range(n):
            for h in range(cap // LANES):
                line = t * (cap // LANES) + h
                ids_o[o, line : line + 1, :] = listed[o : o + 1, h * LANES : (h + 1) * LANES]
    own_ids = pltpu.make_async_copy(ids_o.at[me], ids_s.at[0], load.at[3])
    own_ids.start()
    pl.semaphore_wait(barrier, n + n_table - 2)

    def across(d):
        bit, peer = 1, 0
        while bit < n:
            mine, other = lax.rem(me // bit, 2), lax.rem(d // bit, 2)
            peer += bit * (mine + other - 2 * mine * other)
            bit *= 2
        return peer

    def id_copy(d):
        peer = across(d)
        return push(ids_o.at[peer], ids_v.at[d], id_send.at[0, d], id_recv.at[0, d], "cand", peer)

    def feat_copy(d):
        peer = across(d)
        return push(feats, feats_v.at[me], id_send.at[1, d], id_recv.at[1, d], "cand", peer)

    def row_copy(d):
        peer = across(d)
        from_here = tab_v.at[pl.ds(pl.multiple_of(d * per, per), per), :]
        return push(from_here, blocks.at[place, d], row_send.at[d], row_recv.at[d], "cand", peer)

    def mate_copy(p, d):
        block = blocks.at[p, d]
        return push(block, block, mate_send.at[p, d], mate_recv.at[p, d], "table", mate)

    def level_copy(up, d):
        block = blocks.at[place, d]
        peer = lax.rem(level + up, levels) * CORES + core
        return push(block, block, level_send.at[up, d], level_recv.at[up, d], "table", peer)

    def each(low, high, act):
        def body(d, carry):
            act(d)
            return carry

        lax.fori_loop(low, high, body, 0)

    each(1, n, lambda d: id_copy(d).start())
    spot_copies = [
        push(
            spots.at[place],
            spots.at[place],
            spot_send.at[d],
            spot_recv.at[d],
            "table",
            lax.rem(place + d, n_table),
        )
        for d in range(1, n_table)
    ]
    for copy in spot_copies:
        copy.start()
    each(1, n, lambda d: feat_copy(d).start())
    swaps = [
        push(src, dst, w_send.at[i], w_recv.at[i], "table", mate)
        for i, (src, dst) in enumerate(
            ((first, first_v.at[1]), (second, second_v.at[1]), (bias, biases.at[1]))
        )
    ]
    biases[0] = bias[...]
    feats_v[me] = feats[...]
    tab_copy.wait()
    w_copy.start()
    p_copy.start()
    for copy in held:
        copy.start()
    for copy in swaps:
        copy.start()
    widen(tab_v, wide, tab.shape[0])

    def gather(d, into):
        def body(line, carry):
            at = pl.multiple_of(line * LANES, LANES)
            taken = [ids_s[d, line, j] for j in range(LANES)]
            for b in range(0, LANES, 16):
                values = [wide[pl.ds(row, 1), :] for row in taken[b : b + 16]]
                for j, value in enumerate(values):
                    found[pl.ds(at + b + j, 1), :] = value
            into[pl.ds(at, LANES), :] = found[pl.ds(at, LANES), :].astype(jnp.bfloat16)
            return carry

        lax.fori_loop(0, lines, body, 0)

    def forward(d):
        mate_copy(place, d).start()
        for up in range(1, levels):
            level_copy(up, d).start()

    own_ids.wait()
    gather(0, blocks.at[place, 0])
    forward(0)
    each(1, n, lambda d: id_copy(d).wait_recv())
    to_scalar = pltpu.make_async_copy(
        ids_v.at[pl.ds(1, n - 1)], ids_s.at[pl.ds(1, n - 1)], load.at[4]
    )
    to_scalar.start()
    to_scalar.wait()

    def fill(d):
        gather(d, tab_v.at[pl.ds(pl.multiple_of(d * per, per), per), :])

    def serve(d):
        fill(d)
        row_copy(d).start()

    half = n // 2
    ahead = 2
    serve(half)
    each(1, half, serve)
    each(half + 1, min(half + ahead, n), serve)
    each(half + ahead, n, fill)

    for copy in spot_copies:
        copy.wait()
    for lv in range(levels):
        for j in range(share):
            lists = [
                spots[p, lv * CORES + core, i, j : j + 1, :]
                for p in range(n_table)
                for i in range(tab_dev)
            ]
            at = (lv * share + j) * lanes
            columns[at : at + lanes, 0:tables_all] = jnp.concatenate(lists, axis=0).T
    each(1, n, lambda d: feat_copy(d).wait_recv())
    req_dev = feats.shape[0]
    for c in range(n):
        feats_f[c * req_dev : (c + 1) * req_dev, :] = feats_v[c].astype(jnp.float32)

    def clear(i, carry):
        wide[pl.ds(pl.multiple_of(i * row_all, row_all), row_all), :] = jnp.zeros(
            (row_all, embed), jnp.float32
        )
        return carry

    lax.fori_loop(0, tables_all, clear, 0)
    summed[...] = jnp.zeros_like(summed)
    pieces = n // 2
    deep = w_held.shape[0] // pieces
    part_copies = []
    for d in range(1, n_table):
        peer = lax.rem(place + d, n_table)
        part_copies.append(
            push(
                partial.at[:, lax.rem(peer, CORES)],
                parts.at[place],
                part_send.at[d],
                part_recv.at[d],
                "table",
                peer,
            )
        )
    w_copy.wait()
    p_copy.wait()
    chunk = math.gcd(row_all, 256)
    places = lax.broadcasted_iota(jnp.int32, (chunk, cap), 1).astype(jnp.float32)

    def collect(d):
        begin = (across(d) * cap).astype(jnp.float32)
        for t in range(tables_all):
            block = blocks[t // tab_dev, d, t % tab_dev * cap : (t % tab_dev + 1) * cap, :]

            def body(c, carry):
                at = pl.multiple_of(c * chunk, chunk)
                wanted = columns[pl.ds(at, chunk), t : t + 1] - begin
                hot = jnp.where(places == wanted, 1.0, 0.0).astype(jnp.bfloat16)
                to = pl.ds(pl.multiple_of(t * row_all + at, chunk), chunk)
                wide[to, :] += jnp.dot(hot, block, preferred_element_type=jnp.float32)
                return carry

            lax.fori_loop(0, row_all // chunk, body, 0, unroll=row_all // chunk <= 2)

    def from_levels(d):
        for up in range(1, levels):
            level_copy(up, d).wait_recv()
            mate_copy(lax.rem(level - up + levels, levels) * CORES + core, d).start()

    def from_mate(d):
        for lv in range(levels):
            mate_copy(lv * CORES + 1 - core, d).wait_recv()
        collect(d)

    def step(s, carry):
        @pl.when(s < n)
        def _():
            row_copy(s).wait_recv()
            forward(s)

        @pl.when((s >= half) & (s + ahead < n))
        def _():
            row_copy(s + ahead).start()

        @pl.when(s <= n)
        def _():
            from_levels(s - 1)

        @pl.when(s <= pieces)
        def _():
            at = pl.ds(pl.multiple_of((s - 1) * deep, deep), deep)
            summed[...] += jnp.dot(
                feats_f[:, at].astype(jnp.bfloat16), w_held[at, :], preferred_element_type=jnp.float32
            )

        @pl.when(s == pieces)
        def _():
            tower = jnp.maximum(summed[...] + tower_b[...], 0.0).astype(jnp.bfloat16)
            part = jnp.dot(tower, p_held[...], preferred_element_type=jnp.float32)
            quarter = partial.shape[2]
            for q in range(n_table):
                partial[q // CORES, q % CORES] = part[q * quarter : (q + 1) * quarter, :]
            for copy in part_copies:
                copy.start()
            for y in range(levels):
                parts[place, y] = partial[y, core]

        @pl.when(s >= 2)
        def _():
            from_mate(s - 2)

        return carry

    lax.fori_loop(1, n + 2, step, 0)

    for copy in part_copies + swaps:
        copy.wait()
    for copy in held:
        copy.wait()
    span = max(256, (1 << 18) // rows)
    tile = math.gcd(width, span)
    hidden_tile = math.gcd(first.shape[1], span)
    units, d_top = second.shape
    top_tile = math.gcd(d_top, 256)
    top_copies = []
    for d in range(1, levels + 1):
        at_level = lax.rem(level + d, levels)
        total = parts[0, at_level]
        for q in range(1, n_table):
            total = total + parts[q, at_level]
        proj = total.astype(jnp.bfloat16).astype(jnp.float32)
        for t in range(tables_all):
            lane = slice(t * embed, (t + 1) * embed)
            for r in range(requests):
                at = pl.multiple_of(t * row_all + at_level * rows + r * cand_dev, cand_dev)
                base[r * cand_dev : (r + 1) * cand_dev, lane] = (
                    wide[pl.ds(at, cand_dev), :] + proj[r : r + 1, lane]
                ).astype(jnp.bfloat16)

        def cross(j, carry):
            at = pl.ds(pl.multiple_of(j * tile, tile), tile)
            product = jnp.dot(base[...], cross_v[:, at], preferred_element_type=jnp.float32)
            broad = base[:, at].astype(jnp.float32)
            crossed[:, at] = (broad * (product + cross_b[:, at]) + broad).astype(jnp.bfloat16)
            return carry

        lax.fori_loop(0, width // tile, cross, 0)
        for i in range(CORES):

            def layer(j, carry):
                at = pl.ds(pl.multiple_of(j * hidden_tile, hidden_tile), hidden_tile)
                hidden = jnp.dot(
                    crossed[...], first_v[i, :, at], preferred_element_type=jnp.float32
                )
                hidden = jnp.maximum(hidden + biases[i, :, at], 0.0)
                w_held[i * rows : (i + 1) * rows, at] = hidden.astype(jnp.bfloat16)
                return carry

            lax.fori_loop(0, units // hidden_tile, layer, 0)
        for c in range(d_top // top_tile):
            at = slice(c * top_tile, (c + 1) * top_tile)
            term = jnp.dot(
                w_held[0:rows, 0:units], second_v[0, :, at], preferred_element_type=jnp.float32
            )
            for i in range(1, CORES):
                term += jnp.dot(
                    w_held[i * rows : (i + 1) * rows, 0:units],
                    second_v[i, :, at],
                    preferred_element_type=jnp.float32,
                )
            if d == levels:
                for h in range(top_tile // embed):
                    to = (c * (top_tile // embed) + h) * rows
                    wide[to : to + rows, :] = term[:, h * embed : (h + 1) * embed]
                continue
            sent[d - 1, :, at] = term.astype(jnp.bfloat16)
            top_copies.append(
                push(
                    sent.at[d - 1, :, at],
                    got.at[d - 1, :, at],
                    top_send.at[d - 1, c],
                    top_recv.at[d - 1, c],
                    "table",
                    at_level * CORES + core,
                )
            )
            top_copies[-1].start()

    def drain(d):
        id_copy(d).wait_send()
        feat_copy(d).wait_send()
        row_copy(d).wait_send()

    def drain_blocks(d):
        for lv in range(levels):
            mate_copy(lv * CORES + core, d).wait_send()
        for up in range(1, levels):
            level_copy(up, d).wait_send()

    each(1, n, drain)
    each(0, n, drain_blocks)
    for copy in top_copies:
        copy.wait()
    for c in range(d_top // embed):
        at = slice(c * embed, (c + 1) * embed)
        total = wide[c * rows : (c + 1) * rows, :] + second_b[:, at]
        for d in range(levels - 1):
            total = total + got[d, :, at].astype(jnp.float32)
        crossed[:, at] = jnp.maximum(total, 0.0).astype(jnp.bfloat16)
    for r in range(requests):
        scores = lax.dot_general(
            task_w[...],
            crossed[r * cand_dev : (r + 1) * cand_dev, :],
            (((1,), (1,)), ((), ())),
            preferred_element_type=jnp.float32,
        )
        for k in range(tasks):
            out[k, r : r + 1, :] = scores[k : k + 1, :] + task_b[k]


def on_device(
    user_feats,
    tower_weight,
    tower_bias,
    user_proj,
    item_ids,
    tables,
    cross_weight,
    cross_bias,
    mlp_first,
    first_bias,
    mlp_second,
    second_bias,
    task_weight,
    task_bias,
):
    n_cand = lax.axis_size("cand")
    n_table = lax.axis_size("table")
    tab_dev, requests, cand_dev = item_ids.shape
    rows_dev = tables.shape[1]
    embed = tables.shape[2]
    req_dev, user_width = user_feats.shape
    cap = 2 * req_dev * cand_dev
    row_total = requests * cand_dev
    group = max(1, LANES // cand_dev)
    joined = jnp.concatenate([item_ids[:, g::group] for g in range(group)], axis=-1)
    owner = joined // rows_dev
    local = joined % rows_dev
    steps, lanes = joined.shape[1:]
    per = tab_dev * cap
    lines = per // LANES
    levels = n_table // CORES
    bias_row = first_bias[None, :]
    quarter = requests // n_table
    rows_mine = row_total // n_table
    width = n_table * tab_dev * embed
    parts_shape = (levels, quarter, user_proj.shape[1])
    vmem = pltpu.VMEM
    dma = pltpu.SemaphoreType.DMA
    tasks = task_weight.shape[1]
    d_top = mlp_second.shape[1]
    held_rows = max(tab_dev * rows_dev, n_cand * per)
    wide_rows = max(
        tab_dev * rows_dev, n_table * tab_dev * levels * rows_mine, d_top // embed * rows_mine
    )
    return pl.pallas_call(
        functools.partial(whole_kernel, n_cand, n_table, cap),
        out_shape=jax.ShapeDtypeStruct((tasks, quarter, cand_dev), jnp.float32),
        in_specs=[
            VMEM_SPEC,
            VMEM_SPEC,
            VMEM_SPEC,
            ANY_SPEC,
            ANY_SPEC,
            VMEM_SPEC,
            ANY_SPEC,
            ANY_SPEC,
            ANY_SPEC,
            VMEM_SPEC,
            ANY_SPEC,
            VMEM_SPEC,
            VMEM_SPEC,
            VMEM_SPEC,
            SMEM_SPEC,
        ],
        out_specs=VMEM_SPEC,
        scratch_shapes=[
            vmem((n_cand, lines, LANES), jnp.int32),
            vmem((n_cand, lines, LANES), jnp.int32),
            pltpu.SMEM((n_cand, lines, LANES), jnp.int32),
            vmem((n_table, n_table, tab_dev, steps // n_table, lanes), jnp.float32),
            vmem((levels * rows_mine, LANES), jnp.float32),
            vmem((n_cand, req_dev, user_width), user_feats.dtype),
            vmem((requests, user_width), jnp.float32),
            vmem((held_rows, embed), tables.dtype),
            vmem((wide_rows, embed), jnp.float32),
            vmem((per, embed), jnp.float32),
            vmem((n_table, n_cand, per, embed), tables.dtype),
            vmem((requests, tower_weight.shape[1]), jnp.float32),
            vmem((levels, CORES) + parts_shape[1:], jnp.float32),
            vmem((n_table,) + parts_shape, jnp.float32),
            vmem(tower_weight.shape, tower_weight.dtype),
            vmem(user_proj.shape, user_proj.dtype),
            vmem(cross_weight.shape, cross_weight.dtype),
            vmem((CORES,) + mlp_first.shape, mlp_first.dtype),
            vmem((CORES,) + mlp_second.shape, mlp_second.dtype),
            vmem((CORES,) + bias_row.shape, bias_row.dtype),
            vmem((rows_mine, width), jnp.bfloat16),
            vmem((rows_mine, width), jnp.bfloat16),
            vmem((levels - 1, rows_mine, d_top), jnp.bfloat16),
            vmem((levels - 1, rows_mine, d_top), jnp.bfloat16),
            dma((8,)),
            dma((2, n_cand)),
            dma((2, n_cand)),
            dma((n_table,)),
            dma((n_table,)),
            dma((n_cand,)),
            dma((n_cand,)),
            dma((n_table, n_cand)),
            dma((n_table, n_cand)),
            dma((levels, n_cand)),
            dma((levels, n_cand)),
            dma((3,)),
            dma((3,)),
            dma((n_table,)),
            dma((n_table,)),
            dma((levels - 1, d_top // math.gcd(d_top, 256))),
            dma((levels - 1, d_top // math.gcd(d_top, 256))),
        ],
        compiler_params=pltpu.CompilerParams(
            collective_id=0, has_side_effects=True, vmem_limit_bytes=LIMIT
        ),
        name="whole",
    )(
        owner,
        local,
        user_feats,
        tables.reshape(tab_dev * rows_dev, embed),
        tower_weight,
        tower_bias[None, :],
        user_proj,
        mlp_first,
        mlp_second,
        bias_row,
        cross_weight,
        cross_bias[None, :],
        second_bias[None, :],
        task_weight.T,
        task_bias,
    )


def solution(mesh):
    placed = (
        P("cand", None),
        P(None, "table"),
        P("table"),
        P("table", None),
        P("table", None, "cand"),
        P("table", "cand", None),
        P(),
        P(),
        P(None, "table"),
        P("table"),
        P("table", None),
        P(),
        P(),
        P(),
    )
    return jax.shard_map(
        on_device, mesh=mesh, in_specs=placed, out_specs=P(None, "table", "cand"), check_vma=False
    )
```

```python
import functools
import math

import jax
import jax.numpy as jnp
from jax import lax
from jax.experimental import pallas as pl
from jax.experimental.pallas import tpu as pltpu
from jax.sharding import PartitionSpec as P

MESH = pl.DeviceIdType.MESH
VMEM_SPEC = pl.BlockSpec(memory_space=pltpu.VMEM)
SMEM_SPEC = pl.BlockSpec(memory_space=pltpu.SMEM)
ANY_SPEC = pl.BlockSpec(memory_space=pl.ANY)
CORES = 2
LANES = 128
LIMIT = 62 << 20


def push(src, dst, send, recv, axis, peer):
    return pltpu.make_async_remote_copy(
        src_ref=src,
        dst_ref=dst,
        send_sem=send,
        recv_sem=recv,
        device_id={axis: peer},
        device_id_type=MESH,
    )


def widen(src, dst, rows):
    size = math.gcd(rows, 256)

    def body(i, carry):
        at = pl.multiple_of(i * size, size)
        dst[pl.ds(at, size), :] = src[pl.ds(at, size), :].astype(jnp.float32)
        return carry

    lax.fori_loop(0, rows // size, body, 0)


def whole_kernel(
    n,
    n_table,
    cap,
    rows_dev,
    items,
    feats,
    tab,
    tower_w,
    tower_b,
    proj_w,
    first,
    second,
    bias,
    cross_w,
    cross_b,
    second_b,
    task_w,
    task_b,
    out,
    ids_o,
    ids_v,
    ids_s,
    spots,
    columns,
    feats_v,
    feats_f,
    tab_v,
    wide,
    found,
    blocks,
    summed,
    partial,
    parts,
    w_held,
    p_held,
    cross_v,
    first_v,
    second_v,
    biases,
    base,
    crossed,
    sent,
    got,
    load,
    id_send,
    id_recv,
    spot_send,
    spot_recv,
    row_send,
    row_recv,
    mate_send,
    mate_recv,
    level_send,
    level_recv,
    w_send,
    w_recv,
    part_send,
    part_recv,
    top_send,
    top_recv,
):
    me = lax.axis_index("cand")
    place = lax.axis_index("table")
    core = lax.rem(place, CORES)
    level = place // CORES
    levels = n_table // CORES
    mate = place + 1 - 2 * core
    tab_dev, all_requests, cand_dev = items.shape
    group = max(1, LANES // cand_dev)
    steps, lanes = all_requests // group, group * cand_dev
    per = tab_dev * cap
    lines = per // LANES
    embed = wide.shape[1]
    row_all = columns.shape[0]
    rows, width = base.shape
    tables_all = n_table * tab_dev
    tasks, requests, _ = out.shape

    tab_copy = pltpu.make_async_copy(tab, tab_v.at[pl.ds(0, tab.shape[0]), :], load.at[0])
    w_copy = pltpu.make_async_copy(tower_w, w_held, load.at[1])
    p_copy = pltpu.make_async_copy(proj_w, p_held, load.at[2])
    held = [
        pltpu.make_async_copy(src, dst, load.at[5 + i])
        for i, (src, dst) in enumerate(
            ((cross_w, cross_v), (first, first_v.at[0]), (second, second_v.at[0]))
        )
    ]
    tab_copy.start()
    barrier = pltpu.get_barrier_semaphore()
    for d in range(1, n):
        pl.semaphore_signal(
            barrier, inc=1, device_id={"cand": lax.rem(me + d, n)}, device_id_type=MESH
        )
    for d in range(1, n_table):
        pl.semaphore_signal(
            barrier,
            inc=1,
            device_id={"table": lax.rem(place + d, n_table)},
            device_id_type=MESH,
        )

    owners = lax.broadcasted_iota(jnp.int32, (n, lanes), 0)
    sender = lax.broadcasted_iota(jnp.int32, (lanes, 2 * lanes), 0)
    reader = lax.broadcasted_iota(jnp.int32, (lanes, 2 * lanes), 1)
    counting = jnp.where((sender < reader) | (reader >= lanes), 1.0, 0.0).astype(jnp.bfloat16)
    slots = lax.broadcasted_iota(jnp.int32, (cap, lanes), 0).astype(jnp.float32)
    share = steps // n_table
    for t in range(tab_dev):
        joined = jnp.concatenate(
            [items[t, pl.ds(g, steps, stride=group), :] for g in range(group)], axis=1
        )
        owner = joined // rows_dev
        local = joined - owner * rows_dev
        hots = []
        for j in range(steps):
            hots.append(jnp.where(owner[j : j + 1, :] == owners, 1.0, 0.0))
        counts = jnp.dot(
            jnp.concatenate(hots, axis=0).astype(jnp.bfloat16),
            counting,
            preferred_element_type=jnp.float32,
        )
        before = jnp.zeros((n, lanes), jnp.float32)
        total = jnp.zeros((2 * n, cap), jnp.float32)
        for j in range(steps):
            hot = hots[j]
            mine = counts[j * n : (j + 1) * n, :]
            spot = jnp.sum(hot * (mine[:, 0:lanes] + before), axis=0, keepdims=True)
            before = before + mine[:, lanes:]
            spots[place, j // share, t, j % share : j % share + 1, :] = (
                spot + (owner[j : j + 1, :] * cap).astype(jnp.float32)
            )
            row = local[j : j + 1, :]
            low = (row & (LANES - 1)).astype(jnp.float32)
            high = (row // LANES).astype(jnp.float32)
            digits = jnp.concatenate([hot * low, hot * high], axis=0).astype(jnp.bfloat16)
            at = jnp.where(slots == spot, 1.0, 0.0).astype(jnp.bfloat16)
            total = total + lax.dot_general(
                digits, at, (((1,), (1,)), ((), ())), preferred_element_type=jnp.float32
            )
        listed = (total[0:n] + total[n:] * float(LANES)).astype(jnp.int32) + t * rows_dev
        listed = jnp.minimum(jnp.maximum(listed, 0), tab.shape[0] - 1)
        for o in range(n):
            for h in range(cap // LANES):
                line = t * (cap // LANES) + h
                ids_o[o, line : line + 1, :] = listed[o : o + 1, h * LANES : (h + 1) * LANES]
    own_ids = pltpu.make_async_copy(ids_o.at[me], ids_s.at[0], load.at[3])
    own_ids.start()
    pl.semaphore_wait(barrier, n + n_table - 2)

    def across(d):
        bit, peer = 1, 0
        while bit < n:
            mine, other = lax.rem(me // bit, 2), lax.rem(d // bit, 2)
            peer += bit * (mine + other - 2 * mine * other)
            bit *= 2
        return peer

    def id_copy(d):
        peer = across(d)
        return push(ids_o.at[peer], ids_v.at[d], id_send.at[0, d], id_recv.at[0, d], "cand", peer)

    def feat_copy(d):
        peer = across(d)
        return push(feats, feats_v.at[me], id_send.at[1, d], id_recv.at[1, d], "cand", peer)

    def row_copy(d):
        peer = across(d)
        from_here = tab_v.at[pl.ds(pl.multiple_of(d * per, per), per), :]
        return push(from_here, blocks.at[place, d], row_send.at[d], row_recv.at[d], "cand", peer)

    def mate_copy(p, d):
        block = blocks.at[p, d]
        return push(block, block, mate_send.at[p, d], mate_recv.at[p, d], "table", mate)

    def level_copy(up, d):
        block = blocks.at[place, d]
        peer = lax.rem(level + up, levels) * CORES + core
        return push(block, block, level_send.at[up, d], level_recv.at[up, d], "table", peer)

    def each(low, high, act):
        def body(d, carry):
            act(d)
            return carry

        lax.fori_loop(low, high, body, 0)

    each(1, n, lambda d: id_copy(d).start())
    spot_copies = [
        push(
            spots.at[place],
            spots.at[place],
            spot_send.at[d],
            spot_recv.at[d],
            "table",
            lax.rem(place + d, n_table),
        )
        for d in range(1, n_table)
    ]
    for copy in spot_copies:
        copy.start()
    each(1, n, lambda d: feat_copy(d).start())
    swaps = [
        push(src, dst, w_send.at[i], w_recv.at[i], "table", mate)
        for i, (src, dst) in enumerate(
            ((first, first_v.at[1]), (second, second_v.at[1]), (bias, biases.at[1]))
        )
    ]
    biases[0] = bias[...]
    feats_v[me] = feats[...]
    tab_copy.wait()
    w_copy.start()
    p_copy.start()
    for copy in held:
        copy.start()
    for copy in swaps:
        copy.start()
    widen(tab_v, wide, tab.shape[0])

    def gather(d, into):
        def body(line, carry):
            at = pl.multiple_of(line * LANES, LANES)
            taken = [ids_s[d, line, j] for j in range(LANES)]
            for b in range(0, LANES, 16):
                values = [wide[pl.ds(row, 1), :] for row in taken[b : b + 16]]
                for j, value in enumerate(values):
                    found[pl.ds(at + b + j, 1), :] = value
            into[pl.ds(at, LANES), :] = found[pl.ds(at, LANES), :].astype(jnp.bfloat16)
            return carry

        lax.fori_loop(0, lines, body, 0)

    def forward(d):
        mate_copy(place, d).start()
        for up in range(1, levels):
            level_copy(up, d).start()

    own_ids.wait()
    gather(0, blocks.at[place, 0])
    forward(0)
    each(1, n, lambda d: id_copy(d).wait_recv())
    to_scalar = pltpu.make_async_copy(
        ids_v.at[pl.ds(1, n - 1)], ids_s.at[pl.ds(1, n - 1)], load.at[4]
    )
    to_scalar.start()

    def lender(r):
        return lax.rem(level + r // CORES, levels) * CORES + lax.rem(core + r, CORES)

    for copy in spot_copies:
        copy.wait()
    for lv in range(levels):
        for j in range(share):
            lists = [
                spots[lender(r), lv * CORES + core, i, j : j + 1, :]
                for r in range(n_table)
                for i in range(tab_dev)
            ]
            at = (lv * share + j) * lanes
            columns[at : at + lanes, 0:tables_all] = jnp.concatenate(lists, axis=0).T
    each(1, n, lambda d: feat_copy(d).wait_recv())
    req_dev = feats.shape[0]
    for c in range(n):
        feats_f[c * req_dev : (c + 1) * req_dev, :] = feats_v[c].astype(jnp.float32)

    to_scalar.wait()

    def fill(d):
        gather(d, tab_v.at[pl.ds(pl.multiple_of(d * per, per), per), :])

    def serve(d):
        fill(d)
        row_copy(d).start()

    half = n // 2
    ahead = 2
    serve(1)
    each(half, min(half + 1, n), serve)
    each(2, half, serve)
    each(half + 1, min(half + ahead, n), serve)
    row_copy(1).wait_recv()
    forward(1)
    each(half + ahead, n, fill)

    summed[...] = jnp.zeros_like(summed)
    pieces = n // 2
    deep = w_held.shape[0] // pieces
    part_copies = []
    for d in range(1, n_table):
        peer = lax.rem(place + d, n_table)
        part_copies.append(
            push(
                partial.at[:, lax.rem(peer, CORES)],
                parts.at[place],
                part_send.at[d],
                part_recv.at[d],
                "table",
                peer,
            )
        )
    w_copy.wait()
    p_copy.wait()
    chunk = math.gcd(row_all, 256)
    places = lax.broadcasted_iota(jnp.int32, (chunk, cap), 1).astype(jnp.float32)

    def collect(r, d, fresh=False):
        begin = (across(d) * cap).astype(jnp.float32)
        p = lender(r)
        for i in range(tab_dev):
            block = blocks[p, d, i * cap : (i + 1) * cap, :]
            t = r * tab_dev + i

            def body(c, carry):
                at = pl.multiple_of(c * chunk, chunk)
                wanted = columns[pl.ds(at, chunk), t : t + 1] - begin
                hot = jnp.where(places == wanted, 1.0, 0.0).astype(jnp.bfloat16)
                to = pl.ds(pl.multiple_of((p * tab_dev + i) * row_all + at, chunk), chunk)
                rows_in = jnp.dot(hot, block, preferred_element_type=jnp.float32)
                wide[to, :] = rows_in if fresh else wide[to, :] + rows_in
                return carry

            lax.fori_loop(0, row_all // chunk, body, 0, unroll=row_all // chunk <= 2)

    def near(d, fresh=False):
        collect(0, d, fresh)
        mate_copy(mate, d).wait_recv()
        collect(1, d, fresh)

    def from_levels(d):
        for up in range(1, levels):
            level_copy(up, d).wait_recv()
            mate_copy(lender(CORES * (levels - up)), d).start()

    def far(d, fresh=False):
        for up in range(1, levels):
            collect(CORES * up, d, fresh)

    def far_mates(d, fresh=False):
        for up in range(1, levels):
            mate_copy(lender(CORES * up + 1), d).wait_recv()
            collect(CORES * up + 1, d, fresh)

    def step(s, carry):
        @pl.when((s > 1) & (s < n))
        def _():
            row_copy(s).wait_recv()
            forward(s)

        @pl.when((s >= half) & (s + ahead < n))
        def _():
            row_copy(s + ahead).start()

        @pl.when(s == 1)
        def _():
            near(0, True)

        @pl.when((s > 1) & (s <= n))
        def _():
            near(s - 1)

        @pl.when(s <= n)
        def _():
            from_levels(s - 1)

        @pl.when(s <= pieces)
        def _():
            at = pl.ds(pl.multiple_of((s - 1) * deep, deep), deep)
            summed[...] += jnp.dot(
                feats_f[:, at].astype(jnp.bfloat16), w_held[at, :], preferred_element_type=jnp.float32
            )

        @pl.when(s == pieces)
        def _():
            tower = jnp.maximum(summed[...] + tower_b[...], 0.0).astype(jnp.bfloat16)
            part = jnp.dot(tower, p_held[...], preferred_element_type=jnp.float32)
            quarter = partial.shape[2]
            for q in range(n_table):
                partial[q // CORES, q % CORES] = part[q * quarter : (q + 1) * quarter, :]
            for copy in part_copies:
                copy.start()
            for y in range(levels):
                parts[place, y] = partial[y, core]

        @pl.when(s == 2)
        def _():
            far_mates(0, True)

        @pl.when(s > 2)
        def _():
            far_mates(s - 2)

        @pl.when(s == 1)
        def _():
            far(0, True)

        @pl.when((s > 1) & (s <= n))
        def _():
            far(s - 1)

        return carry

    lax.fori_loop(1, n + 2, step, 0)

    for copy in part_copies + swaps:
        copy.wait()
    for copy in held:
        copy.wait()
    span = max(256, (1 << 18) // rows)
    tile = math.gcd(width, span)
    hidden_tile = math.gcd(first.shape[1], span)
    units, d_top = second.shape
    top_tile = math.gcd(d_top, 256)
    top_copies = []
    for d in range(1, levels + 1):
        at_level = lax.rem(level + d, levels)
        total = parts[0, at_level]
        for q in range(1, n_table):
            total = total + parts[q, at_level]
        proj = total.astype(jnp.bfloat16).astype(jnp.float32)
        for t in range(tables_all):
            lane = slice(t * embed, (t + 1) * embed)
            for r in range(requests):
                at = pl.multiple_of(t * row_all + at_level * rows + r * cand_dev, cand_dev)
                base[r * cand_dev : (r + 1) * cand_dev, lane] = (
                    wide[pl.ds(at, cand_dev), :] + proj[r : r + 1, lane]
                ).astype(jnp.bfloat16)

        def cross(j, carry):
            at = pl.ds(pl.multiple_of(j * tile, tile), tile)
            product = jnp.dot(base[...], cross_v[:, at], preferred_element_type=jnp.float32)
            broad = base[:, at].astype(jnp.float32)
            crossed[:, at] = (broad * (product + cross_b[:, at]) + broad).astype(jnp.bfloat16)
            return carry

        lax.fori_loop(0, width // tile, cross, 0)
        for i in range(CORES):

            def layer(j, carry):
                at = pl.ds(pl.multiple_of(j * hidden_tile, hidden_tile), hidden_tile)
                hidden = jnp.dot(
                    crossed[...], first_v[i, :, at], preferred_element_type=jnp.float32
                )
                hidden = jnp.maximum(hidden + biases[i, :, at], 0.0)
                w_held[i * rows : (i + 1) * rows, at] = hidden.astype(jnp.bfloat16)
                return carry

            lax.fori_loop(0, units // hidden_tile, layer, 0)
        for c in range(d_top // top_tile):
            at = slice(c * top_tile, (c + 1) * top_tile)
            term = jnp.dot(
                w_held[0:rows, 0:units], second_v[0, :, at], preferred_element_type=jnp.float32
            )
            for i in range(1, CORES):
                term += jnp.dot(
                    w_held[i * rows : (i + 1) * rows, 0:units],
                    second_v[i, :, at],
                    preferred_element_type=jnp.float32,
                )
            if d == levels:
                for h in range(top_tile // embed):
                    to = (c * (top_tile // embed) + h) * rows
                    wide[to : to + rows, :] = term[:, h * embed : (h + 1) * embed]
                continue
            sent[d - 1, :, at] = term.astype(jnp.bfloat16)
            top_copies.append(
                push(
                    sent.at[d - 1, :, at],
                    got.at[d - 1, :, at],
                    top_send.at[d - 1, c],
                    top_recv.at[d - 1, c],
                    "table",
                    at_level * CORES + core,
                )
            )
            top_copies[-1].start()

    def drain(d):
        id_copy(d).wait_send()
        feat_copy(d).wait_send()
        row_copy(d).wait_send()

    def drain_blocks(d):
        for lv in range(levels):
            mate_copy(lv * CORES + core, d).wait_send()
        for up in range(1, levels):
            level_copy(up, d).wait_send()

    each(1, n, drain)
    each(0, n, drain_blocks)
    for copy in top_copies:
        copy.wait()
    for c in range(d_top // embed):
        at = slice(c * embed, (c + 1) * embed)
        total = wide[c * rows : (c + 1) * rows, :] + second_b[:, at]
        for d in range(levels - 1):
            total = total + got[d, :, at].astype(jnp.float32)
        crossed[:, at] = jnp.maximum(total, 0.0).astype(jnp.bfloat16)
    for r in range(requests):
        scores = lax.dot_general(
            task_w[...],
            crossed[r * cand_dev : (r + 1) * cand_dev, :],
            (((1,), (1,)), ((), ())),
            preferred_element_type=jnp.float32,
        )
        for k in range(tasks):
            out[k, r : r + 1, :] = scores[k : k + 1, :] + task_b[k]


def on_device(
    user_feats,
    tower_weight,
    tower_bias,
    user_proj,
    item_ids,
    tables,
    cross_weight,
    cross_bias,
    mlp_first,
    first_bias,
    mlp_second,
    second_bias,
    task_weight,
    task_bias,
):
    n_cand = lax.axis_size("cand")
    n_table = lax.axis_size("table")
    tab_dev, requests, cand_dev = item_ids.shape
    rows_dev = tables.shape[1]
    embed = tables.shape[2]
    req_dev, user_width = user_feats.shape
    cap = 2 * req_dev * cand_dev
    row_total = requests * cand_dev
    group = max(1, LANES // cand_dev)
    steps, lanes = requests // group, group * cand_dev
    per = tab_dev * cap
    lines = per // LANES
    levels = n_table // CORES
    bias_row = first_bias[None, :]
    quarter = requests // n_table
    rows_mine = row_total // n_table
    width = n_table * tab_dev * embed
    parts_shape = (levels, quarter, user_proj.shape[1])
    vmem = pltpu.VMEM
    dma = pltpu.SemaphoreType.DMA
    tasks = task_weight.shape[1]
    d_top = mlp_second.shape[1]
    held_rows = max(tab_dev * rows_dev, n_cand * per)
    wide_rows = max(
        tab_dev * rows_dev, n_table * tab_dev * levels * rows_mine, d_top // embed * rows_mine
    )
    return pl.pallas_call(
        functools.partial(whole_kernel, n_cand, n_table, cap, rows_dev),
        out_shape=jax.ShapeDtypeStruct((tasks, quarter, cand_dev), jnp.float32),
        in_specs=[
            VMEM_SPEC,
            VMEM_SPEC,
            ANY_SPEC,
            ANY_SPEC,
            VMEM_SPEC,
            ANY_SPEC,
            ANY_SPEC,
            ANY_SPEC,
            VMEM_SPEC,
            ANY_SPEC,
            VMEM_SPEC,
            VMEM_SPEC,
            VMEM_SPEC,
            SMEM_SPEC,
        ],
        out_specs=VMEM_SPEC,
        scratch_shapes=[
            vmem((n_cand, lines, LANES), jnp.int32),
            vmem((n_cand, lines, LANES), jnp.int32),
            pltpu.SMEM((n_cand, lines, LANES), jnp.int32),
            vmem((n_table, n_table, tab_dev, steps // n_table, lanes), jnp.float32),
            vmem((levels * rows_mine, LANES), jnp.float32),
            vmem((n_cand, req_dev, user_width), user_feats.dtype),
            vmem((requests, user_width), jnp.float32),
            vmem((held_rows, embed), tables.dtype),
            vmem((wide_rows, embed), jnp.float32),
            vmem((per, embed), jnp.float32),
            vmem((n_table, n_cand, per, embed), tables.dtype),
            vmem((requests, tower_weight.shape[1]), jnp.float32),
            vmem((levels, CORES) + parts_shape[1:], jnp.float32),
            vmem((n_table,) + parts_shape, jnp.float32),
            vmem(tower_weight.shape, tower_weight.dtype),
            vmem(user_proj.shape, user_proj.dtype),
            vmem(cross_weight.shape, cross_weight.dtype),
            vmem((CORES,) + mlp_first.shape, mlp_first.dtype),
            vmem((CORES,) + mlp_second.shape, mlp_second.dtype),
            vmem((CORES,) + bias_row.shape, bias_row.dtype),
            vmem((rows_mine, width), jnp.bfloat16),
            vmem((rows_mine, width), jnp.bfloat16),
            vmem((levels - 1, rows_mine, d_top), jnp.bfloat16),
            vmem((levels - 1, rows_mine, d_top), jnp.bfloat16),
            dma((8,)),
            dma((2, n_cand)),
            dma((2, n_cand)),
            dma((n_table,)),
            dma((n_table,)),
            dma((n_cand,)),
            dma((n_cand,)),
            dma((n_table, n_cand)),
            dma((n_table, n_cand)),
            dma((levels, n_cand)),
            dma((levels, n_cand)),
            dma((3,)),
            dma((3,)),
            dma((n_table,)),
            dma((n_table,)),
            dma((levels - 1, d_top // math.gcd(d_top, 256))),
            dma((levels - 1, d_top // math.gcd(d_top, 256))),
        ],
        compiler_params=pltpu.CompilerParams(
            collective_id=0, has_side_effects=True, vmem_limit_bytes=LIMIT
        ),
        name="whole",
    )(
        item_ids,
        user_feats,
        tables.reshape(tab_dev * rows_dev, embed),
        tower_weight,
        tower_bias[None, :],
        user_proj,
        mlp_first,
        mlp_second,
        bias_row,
        cross_weight,
        cross_bias[None, :],
        second_bias[None, :],
        task_weight.T,
        task_bias,
    )


def solution(mesh):
    placed = (
        P("cand", None),
        P(None, "table"),
        P("table"),
        P("table", None),
        P("table", None, "cand"),
        P("table", "cand", None),
        P(),
        P(),
        P(None, "table"),
        P("table"),
        P("table", None),
        P(),
        P(),
        P(),
    )
    return jax.shard_map(
        on_device, mesh=mesh, in_specs=placed, out_specs=P(None, "table", "cand"), check_vma=False
    )
```

```python
import functools
import math

import jax
import jax.numpy as jnp
from jax import lax
from jax.experimental import pallas as pl
from jax.experimental.pallas import tpu as pltpu
from jax.sharding import PartitionSpec as P

MESH = pl.DeviceIdType.MESH
VMEM_SPEC = pl.BlockSpec(memory_space=pltpu.VMEM)
SMEM_SPEC = pl.BlockSpec(memory_space=pltpu.SMEM)
ANY_SPEC = pl.BlockSpec(memory_space=pl.ANY)
CORES = 2
LANES = 128
CUTS = 2
LIMIT = 62 << 20


def push(src, dst, send, recv, axis, peer):
    return pltpu.make_async_remote_copy(
        src_ref=src,
        dst_ref=dst,
        send_sem=send,
        recv_sem=recv,
        device_id={axis: peer},
        device_id_type=MESH,
    )


def widen(src, dst, rows):
    size = math.gcd(rows, 256)

    def body(i, carry):
        at = pl.multiple_of(i * size, size)
        dst[pl.ds(at, size), :] = src[pl.ds(at, size), :].astype(jnp.float32)
        return carry

    lax.fori_loop(0, rows // size, body, 0)


def whole_kernel(
    n,
    n_table,
    cap,
    rows_dev,
    items,
    feats,
    tab,
    tower_w,
    tower_b,
    proj_w,
    first,
    second,
    bias,
    cross_w,
    cross_b,
    second_b,
    task_w,
    task_b,
    out,
    ids_o,
    ids_v,
    ids_s,
    spots,
    columns,
    feats_v,
    feats_f,
    tab_v,
    wide,
    found,
    blocks,
    summed,
    partial,
    parts,
    w_held,
    p_held,
    cross_v,
    first_v,
    second_v,
    biases,
    base,
    crossed,
    sent,
    got,
    load,
    id_send,
    id_recv,
    spot_send,
    spot_recv,
    row_send,
    row_recv,
    mate_send,
    mate_recv,
    level_send,
    level_recv,
    w_send,
    w_recv,
    part_send,
    part_recv,
    top_send,
    top_recv,
):
    me = lax.axis_index("cand")
    place = lax.axis_index("table")
    core = lax.rem(place, CORES)
    level = place // CORES
    levels = n_table // CORES
    mate = place + 1 - 2 * core
    tab_dev, all_requests, cand_dev = items.shape
    group = max(1, LANES // cand_dev)
    steps, lanes = all_requests // group, group * cand_dev
    per = tab_dev * cap
    lines = per // LANES
    embed = wide.shape[1]
    row_all = columns.shape[0]
    rows, width = base.shape
    tables_all = n_table * tab_dev
    tasks, requests, _ = out.shape

    tab_copy = pltpu.make_async_copy(tab, tab_v.at[pl.ds(0, tab.shape[0]), :], load.at[0])
    w_copy = pltpu.make_async_copy(tower_w, w_held, load.at[1])
    p_copy = pltpu.make_async_copy(proj_w, p_held, load.at[2])
    held = [
        pltpu.make_async_copy(src, dst, load.at[5 + i])
        for i, (src, dst) in enumerate(
            ((cross_w, cross_v), (first, first_v.at[0]), (second, second_v.at[0]))
        )
    ]
    tab_copy.start()
    barrier = pltpu.get_barrier_semaphore()
    for d in range(1, n):
        pl.semaphore_signal(
            barrier, inc=1, device_id={"cand": lax.rem(me + d, n)}, device_id_type=MESH
        )
    for d in range(1, n_table):
        pl.semaphore_signal(
            barrier,
            inc=1,
            device_id={"table": lax.rem(place + d, n_table)},
            device_id_type=MESH,
        )

    owners = lax.broadcasted_iota(jnp.int32, (n, lanes), 0)
    sender = lax.broadcasted_iota(jnp.int32, (lanes, 2 * lanes), 0)
    reader = lax.broadcasted_iota(jnp.int32, (lanes, 2 * lanes), 1)
    counting = jnp.where((sender < reader) | (reader >= lanes), 1.0, 0.0).astype(jnp.bfloat16)
    slots = lax.broadcasted_iota(jnp.int32, (cap, lanes), 0).astype(jnp.float32)
    share = steps // n_table
    for t in range(tab_dev):
        joined = jnp.concatenate(
            [items[t, pl.ds(g, steps, stride=group), :] for g in range(group)], axis=1
        )
        owner = joined // rows_dev
        local = joined - owner * rows_dev
        hots = []
        for j in range(steps):
            hots.append(jnp.where(owner[j : j + 1, :] == owners, 1.0, 0.0))
        counts = jnp.dot(
            jnp.concatenate(hots, axis=0).astype(jnp.bfloat16),
            counting,
            preferred_element_type=jnp.float32,
        )
        before = jnp.zeros((n, lanes), jnp.float32)
        total = jnp.zeros((2 * n, cap), jnp.float32)
        for j in range(steps):
            hot = hots[j]
            mine = counts[j * n : (j + 1) * n, :]
            spot = jnp.sum(hot * (mine[:, 0:lanes] + before), axis=0, keepdims=True)
            before = before + mine[:, lanes:]
            spots[place, j // share, t, j % share : j % share + 1, :] = (
                spot + (owner[j : j + 1, :] * cap).astype(jnp.float32)
            )
            row = local[j : j + 1, :]
            low = (row & (LANES - 1)).astype(jnp.float32)
            high = (row // LANES).astype(jnp.float32)
            digits = jnp.concatenate([hot * low, hot * high], axis=0).astype(jnp.bfloat16)
            at = jnp.where(slots == spot, 1.0, 0.0).astype(jnp.bfloat16)
            total = total + lax.dot_general(
                digits, at, (((1,), (1,)), ((), ())), preferred_element_type=jnp.float32
            )
        listed = (total[0:n] + total[n:] * float(LANES)).astype(jnp.int32) + t * rows_dev
        listed = jnp.minimum(jnp.maximum(listed, 0), tab.shape[0] - 1)
        for o in range(n):
            for h in range(cap // LANES):
                line = t * (cap // LANES) + h
                ids_o[o, line : line + 1, :] = listed[o : o + 1, h * LANES : (h + 1) * LANES]
    own_ids = pltpu.make_async_copy(ids_o.at[me], ids_s.at[0], load.at[3])
    own_ids.start()
    pl.semaphore_wait(barrier, n + n_table - 2)

    def across(d):
        bit, peer = 1, 0
        while bit < n:
            mine, other = lax.rem(me // bit, 2), lax.rem(d // bit, 2)
            peer += bit * (mine + other - 2 * mine * other)
            bit *= 2
        return peer

    def id_copy(d):
        peer = across(d)
        return push(ids_o.at[peer], ids_v.at[d], id_send.at[0, d], id_recv.at[0, d], "cand", peer)

    def feat_copy(d):
        peer = across(d)
        return push(feats, feats_v.at[me], id_send.at[1, d], id_recv.at[1, d], "cand", peer)

    def spot_of(d, i):
        return pl.ds(pl.multiple_of(d * per + i * cap, cap), cap)

    def row_copy(d, i):
        peer = across(d)
        to = blocks.at[place, d, pl.ds(i * cap, cap)]
        return push(
            tab_v.at[spot_of(d, i), :], to, row_send.at[d, i], row_recv.at[d, i], "cand", peer
        )

    def mate_copy(p, d, i):
        block = blocks.at[p, d, pl.ds(i * cap, cap)]
        return push(block, block, mate_send.at[p, d, i], mate_recv.at[p, d, i], "table", mate)

    def level_copy(up, d, i):
        block = blocks.at[place, d, pl.ds(i * cap, cap)]
        peer = lax.rem(level + up, levels) * CORES + core
        return push(
            block, block, level_send.at[up, d, i], level_recv.at[up, d, i], "table", peer
        )

    def each(low, high, act):
        def body(d, carry):
            act(d)
            return carry

        lax.fori_loop(low, high, body, 0)

    each(1, n, lambda d: id_copy(d).start())
    spot_copies = [
        push(
            spots.at[place],
            spots.at[place],
            spot_send.at[d],
            spot_recv.at[d],
            "table",
            lax.rem(place + d, n_table),
        )
        for d in range(1, n_table)
    ]
    for copy in spot_copies:
        copy.start()
    each(1, n, lambda d: feat_copy(d).start())
    swaps = [
        push(src, dst, w_send.at[i], w_recv.at[i], "table", mate)
        for i, (src, dst) in enumerate(
            ((first, first_v.at[1]), (second, second_v.at[1]), (bias, biases.at[1]))
        )
    ]
    biases[0] = bias[...]
    feats_v[me] = feats[...]
    tab_copy.wait()
    w_copy.start()
    p_copy.start()
    for copy in held:
        copy.start()
    for copy in swaps:
        copy.start()
    widen(tab_v, wide, tab.shape[0])

    def gather(d, i, into):
        share_of = cap // LANES

        def body(line, carry):
            at = pl.multiple_of(line * LANES, LANES)
            taken = [ids_s[d, i * share_of + line, j] for j in range(LANES)]
            for b in range(0, LANES, 16):
                values = [wide[pl.ds(row, 1), :] for row in taken[b : b + 16]]
                for j, value in enumerate(values):
                    found[pl.ds(at + b + j, 1), :] = value
            into[pl.ds(at, LANES), :] = found[pl.ds(at, LANES), :].astype(jnp.bfloat16)
            return carry

        lax.fori_loop(0, share_of, body, 0)

    def forward(d, i):
        level_starts = [level_copy(up, d, i) for up in range(1, levels)]
        for copy in level_starts:
            copy.start()
        mate_copy(place, d, i).start()

    own_ids.wait()
    for i in range(tab_dev):
        gather(0, i, blocks.at[place, 0, pl.ds(i * cap, cap)])
        forward(0, i)
    each(1, n, lambda d: id_copy(d).wait_recv())
    to_scalar = pltpu.make_async_copy(
        ids_v.at[pl.ds(1, n - 1)], ids_s.at[pl.ds(1, n - 1)], load.at[4]
    )
    to_scalar.start()

    def lender(r):
        return lax.rem(level + r // CORES, levels) * CORES + lax.rem(core + r, CORES)

    for copy in spot_copies:
        copy.wait()
    for lv in range(levels):
        for j in range(share):
            lists = [
                spots[lender(r), lv * CORES + core, i, j : j + 1, :]
                for r in range(n_table)
                for i in range(tab_dev)
            ]
            at = (lv * share + j) * lanes
            columns[at : at + lanes, 0:tables_all] = jnp.concatenate(lists, axis=0).T
    each(1, n, lambda d: feat_copy(d).wait_recv())
    req_dev = feats.shape[0]
    for c in range(n):
        feats_f[c * req_dev : (c + 1) * req_dev, :] = feats_v[c].astype(jnp.float32)

    to_scalar.wait()

    def fill(d):
        for i in range(tab_dev):
            gather(d, i, tab_v.at[spot_of(d, i), :])

    def serve(d):
        for i in range(tab_dev):
            gather(d, i, tab_v.at[spot_of(d, i), :])
            row_copy(d, i).start()

    half = n // 2
    ahead = 2
    each(1, half, serve)
    each(half, min(half + ahead, n), serve)
    for i in range(tab_dev):
        row_copy(1, i).wait_recv()
        forward(1, i)
    each(half + ahead, n, fill)

    summed[...] = jnp.zeros_like(summed)
    pieces = n // 2
    deep = w_held.shape[0] // pieces
    part_copies = []
    for d in range(1, n_table):
        peer = lax.rem(place + d, n_table)
        part_copies.append(
            push(
                partial.at[:, lax.rem(peer, CORES)],
                parts.at[place],
                part_send.at[d],
                part_recv.at[d],
                "table",
                peer,
            )
        )
    w_copy.wait()
    p_copy.wait()
    chunk = math.gcd(row_all, 256)
    compared = jnp.bfloat16 if cap <= 256 else jnp.float32
    places = lax.broadcasted_iota(jnp.int32, (chunk, cap), 1).astype(jnp.float32).astype(compared)
    one, zero = jnp.ones((), compared), jnp.zeros((), compared)

    def collect(r, d, i, fresh):
        begin = (across(d) * cap).astype(jnp.float32)
        p = lender(r)
        block = blocks[p, d, i * cap : (i + 1) * cap, :]
        t = r * tab_dev + i

        def body(c, carry):
            at = pl.multiple_of(c * chunk, chunk)
            wanted = (columns[pl.ds(at, chunk), t : t + 1] - begin).astype(places.dtype)
            hot = jnp.where(places == wanted, one, zero).astype(jnp.bfloat16)
            to = pl.ds(pl.multiple_of((p * tab_dev + i) * row_all + at, chunk), chunk)
            rows_in = jnp.dot(hot, block, preferred_element_type=jnp.float32)
            wide[to, :] = rows_in if fresh else wide[to, :] + rows_in
            return carry

        lax.fori_loop(0, row_all // chunk, body, 0, unroll=row_all // chunk <= 2)

    def near(d, fresh=False):
        for i in range(tab_dev):
            collect(0, d, i, fresh)
            mate_copy(mate, d, i).wait_recv()
            collect(1, d, i, fresh)

    def from_levels(d):
        for i in range(tab_dev):
            for up in range(1, levels):
                level_copy(up, d, i).wait_recv()
                mate_copy(lender(CORES * (levels - up)), d, i).start()

    def far(d, fresh=False):
        for i in range(tab_dev):
            for up in range(1, levels):
                collect(CORES * up, d, i, fresh)

    def far_mates(d, fresh=False):
        for i in range(tab_dev):
            for up in range(1, levels):
                mate_copy(lender(CORES * up + 1), d, i).wait_recv()
                collect(CORES * up + 1, d, i, fresh)

    def step(s, carry):
        for i in range(tab_dev):

            @pl.when((s > 1) & (s < n))
            def _():
                row_copy(s, i).wait_recv()
                forward(s, i)

            @pl.when((s >= half) & (s + ahead < n))
            def _():
                row_copy(s + ahead, i).start()

        @pl.when(s == 1)
        def _():
            near(0, True)

        @pl.when((s > 1) & (s <= n))
        def _():
            near(s - 1)

        @pl.when(s <= n)
        def _():
            from_levels(s - 1)

        @pl.when(s <= pieces)
        def _():
            at = pl.ds(pl.multiple_of((s - 1) * deep, deep), deep)
            summed[...] += jnp.dot(
                feats_f[:, at].astype(jnp.bfloat16), w_held[at, :], preferred_element_type=jnp.float32
            )

        @pl.when(s == pieces)
        def _():
            tower = jnp.maximum(summed[...] + tower_b[...], 0.0).astype(jnp.bfloat16)
            part = jnp.dot(tower, p_held[...], preferred_element_type=jnp.float32)
            quarter = partial.shape[2]
            for q in range(n_table):
                partial[q // CORES, q % CORES] = part[q * quarter : (q + 1) * quarter, :]
            for copy in part_copies:
                copy.start()
            for y in range(levels):
                parts[place, y] = partial[y, core]

        @pl.when(s == 2)
        def _():
            far_mates(0, True)

        @pl.when(s > 2)
        def _():
            far_mates(s - 2)

        @pl.when(s == 1)
        def _():
            far(0, True)

        @pl.when((s > 1) & (s <= n))
        def _():
            far(s - 1)

        return carry

    lax.fori_loop(1, n + 2, step, 0)

    for copy in part_copies + swaps:
        copy.wait()
    for copy in held:
        copy.wait()
    span = max(256, (1 << 18) // rows)
    tile = math.gcd(width, span)
    hidden_tile = math.gcd(first.shape[1], span)
    units, d_top = second.shape
    top_tile = math.gcd(d_top, 256)
    top_copies = []
    for d in range(1, levels + 1):
        at_level = lax.rem(level + d, levels)
        total = parts[0, at_level]
        for q in range(1, n_table):
            total = total + parts[q, at_level]
        proj = total.astype(jnp.bfloat16).astype(jnp.float32)
        cuts = 1 if d == levels else CUTS
        few = rows // cuts
        for cut in range(cuts):
            first_row = cut * few
            mine = slice(first_row, first_row + few)
            for t in range(tables_all):
                lane = slice(t * embed, (t + 1) * embed)
                for r in range(cut * requests // cuts, (cut + 1) * requests // cuts):
                    at = pl.multiple_of(t * row_all + at_level * rows + r * cand_dev, cand_dev)
                    base[r * cand_dev : (r + 1) * cand_dev, lane] = (
                        wide[pl.ds(at, cand_dev), :] + proj[r : r + 1, lane]
                    ).astype(jnp.bfloat16)

            def cross(j, carry):
                at = pl.ds(pl.multiple_of(j * tile, tile), tile)
                product = jnp.dot(base[mine, :], cross_v[:, at], preferred_element_type=jnp.float32)
                broad = base[mine, at].astype(jnp.float32)
                crossed[mine, at] = (broad * (product + cross_b[:, at]) + broad).astype(
                    jnp.bfloat16
                )
                return carry

            lax.fori_loop(0, width // tile, cross, 0)
            for i in range(CORES):

                def layer(j, carry):
                    at = pl.ds(pl.multiple_of(j * hidden_tile, hidden_tile), hidden_tile)
                    hidden = jnp.dot(
                        crossed[mine, :], first_v[i, :, at], preferred_element_type=jnp.float32
                    )
                    hidden = jnp.maximum(hidden + biases[i, :, at], 0.0)
                    start = i * rows + first_row
                    w_held[start : start + few, at] = hidden.astype(jnp.bfloat16)
                    return carry

                lax.fori_loop(0, units // hidden_tile, layer, 0)
            for c in range(d_top // top_tile):
                at = slice(c * top_tile, (c + 1) * top_tile)
                term = jnp.dot(
                    w_held[mine, 0:units], second_v[0, :, at], preferred_element_type=jnp.float32
                )
                for i in range(1, CORES):
                    term += jnp.dot(
                        w_held[i * rows + first_row : i * rows + first_row + few, 0:units],
                        second_v[i, :, at],
                        preferred_element_type=jnp.float32,
                    )
                if d == levels:
                    for h in range(top_tile // embed):
                        to = (c * (top_tile // embed) + h) * rows
                        wide[to : to + rows, :] = term[:, h * embed : (h + 1) * embed]
                    continue
                sent[d - 1, mine, at] = term.astype(jnp.bfloat16)
                top_copies.append(
                    push(
                        sent.at[d - 1, mine, at],
                        got.at[d - 1, mine, at],
                        top_send.at[d - 1, cut, c],
                        top_recv.at[d - 1, cut, c],
                        "table",
                        at_level * CORES + core,
                    )
                )
                top_copies[-1].start()

    def drain(d):
        id_copy(d).wait_send()
        feat_copy(d).wait_send()
        for i in range(tab_dev):
            row_copy(d, i).wait_send()

    def drain_blocks(d):
        for i in range(tab_dev):
            for lv in range(levels):
                mate_copy(lv * CORES + core, d, i).wait_send()
            for up in range(1, levels):
                level_copy(up, d, i).wait_send()

    each(1, n, drain)
    each(0, n, drain_blocks)
    for copy in top_copies:
        copy.wait()
    for c in range(d_top // embed):
        at = slice(c * embed, (c + 1) * embed)
        total = wide[c * rows : (c + 1) * rows, :] + second_b[:, at]
        for d in range(levels - 1):
            total = total + got[d, :, at].astype(jnp.float32)
        crossed[:, at] = jnp.maximum(total, 0.0).astype(jnp.bfloat16)
    for r in range(requests):
        scores = lax.dot_general(
            task_w[...],
            crossed[r * cand_dev : (r + 1) * cand_dev, :],
            (((1,), (1,)), ((), ())),
            preferred_element_type=jnp.float32,
        )
        for k in range(tasks):
            out[k, r : r + 1, :] = scores[k : k + 1, :] + task_b[k]


def on_device(
    user_feats,
    tower_weight,
    tower_bias,
    user_proj,
    item_ids,
    tables,
    cross_weight,
    cross_bias,
    mlp_first,
    first_bias,
    mlp_second,
    second_bias,
    task_weight,
    task_bias,
):
    n_cand = lax.axis_size("cand")
    n_table = lax.axis_size("table")
    tab_dev, requests, cand_dev = item_ids.shape
    rows_dev = tables.shape[1]
    embed = tables.shape[2]
    req_dev, user_width = user_feats.shape
    cap = 2 * req_dev * cand_dev
    row_total = requests * cand_dev
    group = max(1, LANES // cand_dev)
    steps, lanes = requests // group, group * cand_dev
    per = tab_dev * cap
    lines = per // LANES
    levels = n_table // CORES
    bias_row = first_bias[None, :]
    quarter = requests // n_table
    rows_mine = row_total // n_table
    width = n_table * tab_dev * embed
    parts_shape = (levels, quarter, user_proj.shape[1])
    vmem = pltpu.VMEM
    dma = pltpu.SemaphoreType.DMA
    tasks = task_weight.shape[1]
    d_top = mlp_second.shape[1]
    held_rows = max(tab_dev * rows_dev, n_cand * per)
    wide_rows = max(
        tab_dev * rows_dev, n_table * tab_dev * levels * rows_mine, d_top // embed * rows_mine
    )
    return pl.pallas_call(
        functools.partial(whole_kernel, n_cand, n_table, cap, rows_dev),
        out_shape=jax.ShapeDtypeStruct((tasks, quarter, cand_dev), jnp.float32),
        in_specs=[
            VMEM_SPEC,
            VMEM_SPEC,
            ANY_SPEC,
            ANY_SPEC,
            VMEM_SPEC,
            ANY_SPEC,
            ANY_SPEC,
            ANY_SPEC,
            VMEM_SPEC,
            ANY_SPEC,
            VMEM_SPEC,
            VMEM_SPEC,
            VMEM_SPEC,
            SMEM_SPEC,
        ],
        out_specs=VMEM_SPEC,
        scratch_shapes=[
            vmem((n_cand, lines, LANES), jnp.int32),
            vmem((n_cand, lines, LANES), jnp.int32),
            pltpu.SMEM((n_cand, lines, LANES), jnp.int32),
            vmem((n_table, n_table, tab_dev, steps // n_table, lanes), jnp.float32),
            vmem((levels * rows_mine, LANES), jnp.float32),
            vmem((n_cand, req_dev, user_width), user_feats.dtype),
            vmem((requests, user_width), jnp.float32),
            vmem((held_rows, embed), tables.dtype),
            vmem((wide_rows, embed), jnp.float32),
            vmem((per, embed), jnp.float32),
            vmem((n_table, n_cand, per, embed), tables.dtype),
            vmem((requests, tower_weight.shape[1]), jnp.float32),
            vmem((levels, CORES) + parts_shape[1:], jnp.float32),
            vmem((n_table,) + parts_shape, jnp.float32),
            vmem(tower_weight.shape, tower_weight.dtype),
            vmem(user_proj.shape, user_proj.dtype),
            vmem(cross_weight.shape, cross_weight.dtype),
            vmem((CORES,) + mlp_first.shape, mlp_first.dtype),
            vmem((CORES,) + mlp_second.shape, mlp_second.dtype),
            vmem((CORES,) + bias_row.shape, bias_row.dtype),
            vmem((rows_mine, width), jnp.bfloat16),
            vmem((rows_mine, width), jnp.bfloat16),
            vmem((levels - 1, rows_mine, d_top), jnp.bfloat16),
            vmem((levels - 1, rows_mine, d_top), jnp.bfloat16),
            dma((8,)),
            dma((2, n_cand)),
            dma((2, n_cand)),
            dma((n_table,)),
            dma((n_table,)),
            dma((n_cand, tab_dev)),
            dma((n_cand, tab_dev)),
            dma((n_table, n_cand, tab_dev)),
            dma((n_table, n_cand, tab_dev)),
            dma((levels, n_cand, tab_dev)),
            dma((levels, n_cand, tab_dev)),
            dma((3,)),
            dma((3,)),
            dma((n_table,)),
            dma((n_table,)),
            dma((levels - 1, CUTS, d_top // math.gcd(d_top, 256))),
            dma((levels - 1, CUTS, d_top // math.gcd(d_top, 256))),
        ],
        compiler_params=pltpu.CompilerParams(
            collective_id=0, has_side_effects=True, vmem_limit_bytes=LIMIT
        ),
        name="whole",
    )(
        item_ids,
        user_feats,
        tables.reshape(tab_dev * rows_dev, embed),
        tower_weight,
        tower_bias[None, :],
        user_proj,
        mlp_first,
        mlp_second,
        bias_row,
        cross_weight,
        cross_bias[None, :],
        second_bias[None, :],
        task_weight.T,
        task_bias,
    )


def solution(mesh):
    placed = (
        P("cand", None),
        P(None, "table"),
        P("table"),
        P("table", None),
        P("table", None, "cand"),
        P("table", "cand", None),
        P(),
        P(),
        P(None, "table"),
        P("table"),
        P("table", None),
        P(),
        P(),
        P(),
    )
    return jax.shard_map(
        on_device, mesh=mesh, in_specs=placed, out_specs=P(None, "table", "cand"), check_vma=False
    )
```

```python
import functools
import math

import jax
import jax.numpy as jnp
from jax import lax
from jax.experimental import pallas as pl
from jax.experimental.pallas import tpu as pltpu
from jax.sharding import PartitionSpec as P

MESH = pl.DeviceIdType.MESH
VMEM_SPEC = pl.BlockSpec(memory_space=pltpu.VMEM)
SMEM_SPEC = pl.BlockSpec(memory_space=pltpu.SMEM)
ANY_SPEC = pl.BlockSpec(memory_space=pl.ANY)
CORES = 2
LANES = 128
CUTS = 2
LIMIT = 62 << 20


def push(src, dst, send, recv, axis, peer):
    return pltpu.make_async_remote_copy(
        src_ref=src,
        dst_ref=dst,
        send_sem=send,
        recv_sem=recv,
        device_id={axis: peer},
        device_id_type=MESH,
    )


def widen(src, dst, rows):
    size = math.gcd(rows, 256)

    def body(i, carry):
        at = pl.multiple_of(i * size, size)
        dst[pl.ds(at, size), :] = src[pl.ds(at, size), :].astype(jnp.float32)
        return carry

    lax.fori_loop(0, rows // size, body, 0)


def whole_kernel(
    n,
    n_table,
    cap,
    rows_dev,
    items,
    feats,
    tab,
    tower_w,
    tower_b,
    proj_w,
    first,
    second,
    bias,
    cross_w,
    cross_b,
    second_b,
    task_w,
    task_b,
    out,
    ids_o,
    ids_v,
    ids_s,
    spots,
    columns,
    feats_v,
    feats_f,
    tab_v,
    wide,
    found,
    blocks,
    summed,
    partial,
    parts,
    w_held,
    p_held,
    cross_v,
    first_v,
    second_v,
    biases,
    base,
    crossed,
    sent,
    got,
    load,
    id_send,
    id_recv,
    spot_send,
    spot_recv,
    row_send,
    row_recv,
    mate_send,
    mate_recv,
    level_send,
    level_recv,
    w_send,
    w_recv,
    part_send,
    part_recv,
    top_send,
    top_recv,
):
    me = lax.axis_index("cand")
    place = lax.axis_index("table")
    core = lax.rem(place, CORES)
    level = place // CORES
    levels = n_table // CORES
    mate = place + 1 - 2 * core
    tab_dev, all_requests, cand_dev = items.shape
    group = max(1, LANES // cand_dev)
    steps, lanes = all_requests // group, group * cand_dev
    per = tab_dev * cap
    lines = per // LANES
    embed = wide.shape[1]
    row_all = columns.shape[0]
    rows, width = base.shape
    tables_all = n_table * tab_dev
    tasks, requests, _ = out.shape

    tab_copy = pltpu.make_async_copy(tab, tab_v.at[pl.ds(0, tab.shape[0]), :], load.at[0])
    w_copy = pltpu.make_async_copy(tower_w, w_held, load.at[1])
    p_copy = pltpu.make_async_copy(proj_w, p_held, load.at[2])
    held = [
        pltpu.make_async_copy(src, dst, load.at[5 + i])
        for i, (src, dst) in enumerate(
            ((cross_w, cross_v), (first, first_v.at[0]), (second, second_v.at[0]))
        )
    ]
    tab_copy.start()
    barrier = pltpu.get_barrier_semaphore()
    for d in range(1, n):
        pl.semaphore_signal(
            barrier, inc=1, device_id={"cand": lax.rem(me + d, n)}, device_id_type=MESH
        )
    for d in range(1, n_table):
        pl.semaphore_signal(
            barrier,
            inc=1,
            device_id={"table": lax.rem(place + d, n_table)},
            device_id_type=MESH,
        )

    owners = lax.broadcasted_iota(jnp.int32, (n, lanes), 0)
    sender = lax.broadcasted_iota(jnp.int32, (lanes, 2 * lanes), 0)
    reader = lax.broadcasted_iota(jnp.int32, (lanes, 2 * lanes), 1)
    counting = jnp.where((sender < reader) | (reader >= lanes), 1.0, 0.0).astype(jnp.bfloat16)
    slots = lax.broadcasted_iota(jnp.int32, (cap, lanes), 0).astype(jnp.float32)
    share = steps // n_table
    for t in range(tab_dev):
        joined = jnp.concatenate(
            [items[t, pl.ds(g, steps, stride=group), :] for g in range(group)], axis=1
        )
        owner = joined // rows_dev
        local = joined - owner * rows_dev
        hots = []
        for j in range(steps):
            hots.append(jnp.where(owner[j : j + 1, :] == owners, 1.0, 0.0))
        counts = jnp.dot(
            jnp.concatenate(hots, axis=0).astype(jnp.bfloat16),
            counting,
            preferred_element_type=jnp.float32,
        )
        before = jnp.zeros((n, lanes), jnp.float32)
        total = jnp.zeros((2 * n, cap), jnp.float32)
        for j in range(steps):
            hot = hots[j]
            mine = counts[j * n : (j + 1) * n, :]
            spot = jnp.sum(hot * (mine[:, 0:lanes] + before), axis=0, keepdims=True)
            before = before + mine[:, lanes:]
            spots[place, j // share, t, j % share : j % share + 1, :] = (
                spot + (owner[j : j + 1, :] * cap).astype(jnp.float32)
            )
            row = local[j : j + 1, :]
            low = (row & (LANES - 1)).astype(jnp.float32)
            high = (row // LANES).astype(jnp.float32)
            digits = jnp.concatenate([hot * low, hot * high], axis=0).astype(jnp.bfloat16)
            at = jnp.where(slots == spot, 1.0, 0.0).astype(jnp.bfloat16)
            total = total + lax.dot_general(
                digits, at, (((1,), (1,)), ((), ())), preferred_element_type=jnp.float32
            )
        listed = (total[0:n] + total[n:] * float(LANES)).astype(jnp.int32) + t * rows_dev
        listed = jnp.minimum(jnp.maximum(listed, 0), tab.shape[0] - 1)
        for o in range(n):
            for h in range(cap // LANES):
                line = t * (cap // LANES) + h
                ids_o[o, line : line + 1, :] = listed[o : o + 1, h * LANES : (h + 1) * LANES]
    own_ids = pltpu.make_async_copy(ids_o.at[me], ids_s.at[0], load.at[3])
    own_ids.start()
    pl.semaphore_wait(barrier, n + n_table - 2)

    def across(d):
        bit, peer = 1, 0
        while bit < n:
            mine, other = lax.rem(me // bit, 2), lax.rem(d // bit, 2)
            peer += bit * (mine + other - 2 * mine * other)
            bit *= 2
        return peer

    def id_copy(d):
        peer = across(d)
        return push(ids_o.at[peer], ids_v.at[d], id_send.at[0, d], id_recv.at[0, d], "cand", peer)

    def feat_copy(d):
        peer = across(d)
        return push(feats, feats_v.at[me], id_send.at[1, d], id_recv.at[1, d], "cand", peer)

    def spot_of(d, i):
        return pl.ds(pl.multiple_of(d * per + i * cap, cap), cap)

    def row_copy(d, i):
        peer = across(d)
        to = blocks.at[place, d, pl.ds(i * cap, cap)]
        return push(
            tab_v.at[spot_of(d, i), :], to, row_send.at[d, i], row_recv.at[d, i], "cand", peer
        )

    def mate_copy(p, d, i):
        block = blocks.at[p, d, pl.ds(i * cap, cap)]
        return push(block, block, mate_send.at[p, d, i], mate_recv.at[p, d, i], "table", mate)

    def level_copy(up, d, i):
        block = blocks.at[place, d, pl.ds(i * cap, cap)]
        peer = lax.rem(level + up, levels) * CORES + core
        return push(
            block, block, level_send.at[up, d, i], level_recv.at[up, d, i], "table", peer
        )

    def each(low, high, act):
        def body(d, carry):
            act(d)
            return carry

        lax.fori_loop(low, high, body, 0)

    each(1, n, lambda d: id_copy(d).start())
    spot_copies = [
        push(
            spots.at[place],
            spots.at[place],
            spot_send.at[d],
            spot_recv.at[d],
            "table",
            lax.rem(place + d, n_table),
        )
        for d in range(1, n_table)
    ]
    for copy in spot_copies:
        copy.start()
    each(1, n, lambda d: feat_copy(d).start())
    swaps = [
        push(src, dst, w_send.at[i], w_recv.at[i], "table", mate)
        for i, (src, dst) in enumerate(
            ((first, first_v.at[1]), (second, second_v.at[1]), (bias, biases.at[1]))
        )
    ]
    biases[0] = bias[...]
    feats_v[me] = feats[...]
    tab_copy.wait()
    w_copy.start()
    p_copy.start()
    for copy in held:
        copy.start()
    for copy in swaps:
        copy.start()
    widen(tab_v, wide, tab.shape[0])

    def gather(d, i, into):
        share_of = cap // LANES

        def body(line, carry):
            at = pl.multiple_of(line * LANES, LANES)
            taken = [ids_s[d, i * share_of + line, j] for j in range(LANES)]
            for b in range(0, LANES, 16):
                values = [wide[pl.ds(row, 1), :] for row in taken[b : b + 16]]
                for j, value in enumerate(values):
                    found[pl.ds(at + b + j, 1), :] = value
            into[pl.ds(at, LANES), :] = found[pl.ds(at, LANES), :].astype(jnp.bfloat16)
            return carry

        lax.fori_loop(0, share_of, body, 0)

    def forward(d, i):
        level_starts = [level_copy(up, d, i) for up in range(1, levels)]
        for copy in level_starts:
            copy.start()
        mate_copy(place, d, i).start()

    own_ids.wait()
    for i in range(tab_dev):
        gather(0, i, blocks.at[place, 0, pl.ds(i * cap, cap)])
        forward(0, i)
    each(1, n, lambda d: id_copy(d).wait_recv())
    to_scalar = pltpu.make_async_copy(
        ids_v.at[pl.ds(1, n - 1)], ids_s.at[pl.ds(1, n - 1)], load.at[4]
    )
    to_scalar.start()

    def lender(r):
        return lax.rem(level + r // CORES, levels) * CORES + lax.rem(core + r, CORES)

    for copy in spot_copies:
        copy.wait()
    for lv in range(levels):
        for j in range(share):
            lists = [
                spots[lender(r), lv * CORES + core, i, j : j + 1, :]
                for r in range(n_table)
                for i in range(tab_dev)
            ]
            at = (lv * share + j) * lanes
            columns[at : at + lanes, 0:tables_all] = jnp.concatenate(lists, axis=0).T
    each(1, n, lambda d: feat_copy(d).wait_recv())
    req_dev = feats.shape[0]
    for c in range(n):
        feats_f[c * req_dev : (c + 1) * req_dev, :] = feats_v[c].astype(jnp.float32)

    to_scalar.wait()

    def fill(d):
        for i in range(tab_dev):
            gather(d, i, tab_v.at[spot_of(d, i), :])

    def serve(d):
        for i in range(tab_dev):
            gather(d, i, tab_v.at[spot_of(d, i), :])
            row_copy(d, i).start()

    half = n // 2
    ahead = 2
    each(1, half, serve)
    each(half, min(half + ahead, n), serve)
    for i in range(tab_dev):
        row_copy(1, i).wait_recv()
        forward(1, i)
    each(half + ahead, n, fill)

    summed[...] = jnp.zeros_like(summed)
    pieces = n // 2
    deep = w_held.shape[0] // pieces
    part_copies = []
    for d in range(1, n_table):
        peer = lax.rem(place + d, n_table)
        part_copies.append(
            push(
                partial.at[:, lax.rem(peer, CORES)],
                parts.at[place],
                part_send.at[d],
                part_recv.at[d],
                "table",
                peer,
            )
        )
    w_copy.wait()
    p_copy.wait()
    chunk = math.gcd(row_all, 256)
    compared = jnp.bfloat16 if cap <= 256 else jnp.float32
    places = lax.broadcasted_iota(jnp.int32, (chunk, cap), 1).astype(jnp.float32).astype(compared)
    one, zero = jnp.ones((), compared), jnp.zeros((), compared)

    def collect(r, d, i, fresh):
        begin = (across(d) * cap).astype(jnp.float32)
        p = lender(r)
        block = blocks[p, d, i * cap : (i + 1) * cap, :]
        t = r * tab_dev + i

        def body(c, carry):
            at = pl.multiple_of(c * chunk, chunk)
            wanted = (columns[pl.ds(at, chunk), t : t + 1] - begin).astype(places.dtype)
            hot = jnp.where(places == wanted, one, zero).astype(jnp.bfloat16)
            to = pl.ds(pl.multiple_of((p * tab_dev + i) * row_all + at, chunk), chunk)
            rows_in = jnp.dot(hot, block, preferred_element_type=jnp.float32)
            wide[to, :] = rows_in if fresh else wide[to, :] + rows_in
            return carry

        lax.fori_loop(0, row_all // chunk, body, 0, unroll=row_all // chunk <= 2)

    def near(d, fresh=False):
        for i in range(tab_dev):
            collect(0, d, i, fresh)
            mate_copy(mate, d, i).wait_recv()
            collect(1, d, i, fresh)

    def from_levels(d):
        for i in range(tab_dev):
            for up in range(1, levels):
                level_copy(up, d, i).wait_recv()
                mate_copy(lender(CORES * (levels - up)), d, i).start()

    def far(d, fresh=False):
        for i in range(tab_dev):
            for up in range(1, levels):
                collect(CORES * up, d, i, fresh)

    def far_mates(d, fresh=False):
        for i in range(tab_dev):
            for up in range(1, levels):
                mate_copy(lender(CORES * up + 1), d, i).wait_recv()
                collect(CORES * up + 1, d, i, fresh)

    def step(s, carry):
        for i in range(tab_dev):

            @pl.when((s > 1) & (s < n))
            def _():
                row_copy(s, i).wait_recv()
                forward(s, i)

            @pl.when((s >= half) & (s + ahead < n))
            def _():
                row_copy(s + ahead, i).start()

        @pl.when(s == 1)
        def _():
            near(0, True)

        @pl.when((s > 1) & (s <= n))
        def _():
            near(s - 1)

        @pl.when((s >= 2) & (s <= n + 1))
        def _():
            from_levels(s - 2)

        @pl.when(s <= pieces)
        def _():
            at = pl.ds(pl.multiple_of((s - 1) * deep, deep), deep)
            summed[...] += jnp.dot(
                feats_f[:, at].astype(jnp.bfloat16), w_held[at, :], preferred_element_type=jnp.float32
            )

        @pl.when(s == pieces)
        def _():
            tower = jnp.maximum(summed[...] + tower_b[...], 0.0).astype(jnp.bfloat16)
            part = jnp.dot(tower, p_held[...], preferred_element_type=jnp.float32)
            quarter = partial.shape[2]
            for q in range(n_table):
                partial[q // CORES, q % CORES] = part[q * quarter : (q + 1) * quarter, :]
            for copy in part_copies:
                copy.start()
            for y in range(levels):
                parts[place, y] = partial[y, core]

        @pl.when(s == 3)
        def _():
            far_mates(0, True)

        @pl.when(s > 3)
        def _():
            far_mates(s - 3)

        @pl.when(s == 2)
        def _():
            far(0, True)

        @pl.when((s > 2) & (s <= n + 1))
        def _():
            far(s - 2)

        return carry

    lax.fori_loop(1, n + 3, step, 0)

    for copy in part_copies + swaps:
        copy.wait()
    for copy in held:
        copy.wait()
    span = max(256, (1 << 18) // rows)
    tile = math.gcd(width, span)
    hidden_tile = math.gcd(first.shape[1], span)
    units, d_top = second.shape
    top_tile = math.gcd(d_top, 512)
    top_copies = []
    for d in range(1, levels + 1):
        at_level = lax.rem(level + d, levels)
        total = parts[0, at_level]
        for q in range(1, n_table):
            total = total + parts[q, at_level]
        proj = total.astype(jnp.bfloat16).astype(jnp.float32)
        cuts = 1 if d == levels else CUTS
        few = rows // cuts
        for cut in range(cuts):
            first_row = cut * few
            mine = slice(first_row, first_row + few)
            for t in range(tables_all):
                lane = slice(t * embed, (t + 1) * embed)
                for r in range(cut * requests // cuts, (cut + 1) * requests // cuts):
                    at = pl.multiple_of(t * row_all + at_level * rows + r * cand_dev, cand_dev)
                    base[r * cand_dev : (r + 1) * cand_dev, lane] = (
                        wide[pl.ds(at, cand_dev), :] + proj[r : r + 1, lane]
                    ).astype(jnp.bfloat16)

            def cross(j, carry):
                at = pl.ds(pl.multiple_of(j * tile, tile), tile)
                product = jnp.dot(base[mine, :], cross_v[:, at], preferred_element_type=jnp.float32)
                broad = base[mine, at].astype(jnp.float32)
                crossed[mine, at] = (broad * (product + cross_b[:, at]) + broad).astype(
                    jnp.bfloat16
                )
                return carry

            lax.fori_loop(0, width // tile, cross, 0)
            for i in range(CORES):

                def layer(j, carry):
                    at = pl.ds(pl.multiple_of(j * hidden_tile, hidden_tile), hidden_tile)
                    hidden = jnp.dot(
                        crossed[mine, :], first_v[i, :, at], preferred_element_type=jnp.float32
                    )
                    hidden = jnp.maximum(hidden + biases[i, :, at], 0.0)
                    start = i * rows + first_row
                    w_held[start : start + few, at] = hidden.astype(jnp.bfloat16)
                    return carry

                lax.fori_loop(0, units // hidden_tile, layer, 0)
            for c in range(d_top // top_tile):
                at = slice(c * top_tile, (c + 1) * top_tile)
                term = jnp.dot(
                    w_held[mine, 0:units], second_v[0, :, at], preferred_element_type=jnp.float32
                )
                for i in range(1, CORES):
                    term += jnp.dot(
                        w_held[i * rows + first_row : i * rows + first_row + few, 0:units],
                        second_v[i, :, at],
                        preferred_element_type=jnp.float32,
                    )
                if d == levels:
                    for h in range(top_tile // embed):
                        to = (c * (top_tile // embed) + h) * rows
                        wide[to : to + rows, :] = term[:, h * embed : (h + 1) * embed]
                    continue
                sent[d - 1, mine, at] = term.astype(jnp.bfloat16)
                top_copies.append(
                    push(
                        sent.at[d - 1, mine, at],
                        got.at[d - 1, mine, at],
                        top_send.at[d - 1, cut, c],
                        top_recv.at[d - 1, cut, c],
                        "table",
                        at_level * CORES + core,
                    )
                )
                top_copies[-1].start()

    def drain(d):
        id_copy(d).wait_send()
        feat_copy(d).wait_send()
        for i in range(tab_dev):
            row_copy(d, i).wait_send()

    def drain_blocks(d):
        for i in range(tab_dev):
            for lv in range(levels):
                mate_copy(lv * CORES + core, d, i).wait_send()
            for up in range(1, levels):
                level_copy(up, d, i).wait_send()

    each(1, n, drain)
    each(0, n, drain_blocks)
    for copy in top_copies:
        copy.wait()
    for c in range(d_top // embed):
        at = slice(c * embed, (c + 1) * embed)
        total = wide[c * rows : (c + 1) * rows, :] + second_b[:, at]
        for d in range(levels - 1):
            total = total + got[d, :, at].astype(jnp.float32)
        crossed[:, at] = jnp.maximum(total, 0.0).astype(jnp.bfloat16)
    for r in range(requests):
        scores = lax.dot_general(
            task_w[...],
            crossed[r * cand_dev : (r + 1) * cand_dev, :],
            (((1,), (1,)), ((), ())),
            preferred_element_type=jnp.float32,
        )
        for k in range(tasks):
            out[k, r : r + 1, :] = scores[k : k + 1, :] + task_b[k]


def on_device(
    user_feats,
    tower_weight,
    tower_bias,
    user_proj,
    item_ids,
    tables,
    cross_weight,
    cross_bias,
    mlp_first,
    first_bias,
    mlp_second,
    second_bias,
    task_weight,
    task_bias,
):
    n_cand = lax.axis_size("cand")
    n_table = lax.axis_size("table")
    tab_dev, requests, cand_dev = item_ids.shape
    rows_dev = tables.shape[1]
    embed = tables.shape[2]
    req_dev, user_width = user_feats.shape
    cap = 2 * req_dev * cand_dev
    row_total = requests * cand_dev
    group = max(1, LANES // cand_dev)
    steps, lanes = requests // group, group * cand_dev
    per = tab_dev * cap
    lines = per // LANES
    levels = n_table // CORES
    bias_row = first_bias[None, :]
    quarter = requests // n_table
    rows_mine = row_total // n_table
    width = n_table * tab_dev * embed
    parts_shape = (levels, quarter, user_proj.shape[1])
    vmem = pltpu.VMEM
    dma = pltpu.SemaphoreType.DMA
    tasks = task_weight.shape[1]
    d_top = mlp_second.shape[1]
    held_rows = max(tab_dev * rows_dev, n_cand * per)
    wide_rows = max(
        tab_dev * rows_dev, n_table * tab_dev * levels * rows_mine, d_top // embed * rows_mine
    )
    return pl.pallas_call(
        functools.partial(whole_kernel, n_cand, n_table, cap, rows_dev),
        out_shape=jax.ShapeDtypeStruct((tasks, quarter, cand_dev), jnp.float32),
        in_specs=[
            VMEM_SPEC,
            VMEM_SPEC,
            ANY_SPEC,
            ANY_SPEC,
            VMEM_SPEC,
            ANY_SPEC,
            ANY_SPEC,
            ANY_SPEC,
            VMEM_SPEC,
            ANY_SPEC,
            VMEM_SPEC,
            VMEM_SPEC,
            VMEM_SPEC,
            SMEM_SPEC,
        ],
        out_specs=VMEM_SPEC,
        scratch_shapes=[
            vmem((n_cand, lines, LANES), jnp.int32),
            vmem((n_cand, lines, LANES), jnp.int32),
            pltpu.SMEM((n_cand, lines, LANES), jnp.int32),
            vmem((n_table, n_table, tab_dev, steps // n_table, lanes), jnp.float32),
            vmem((levels * rows_mine, LANES), jnp.float32),
            vmem((n_cand, req_dev, user_width), user_feats.dtype),
            vmem((requests, user_width), jnp.float32),
            vmem((held_rows, embed), tables.dtype),
            vmem((wide_rows, embed), jnp.float32),
            vmem((per, embed), jnp.float32),
            vmem((n_table, n_cand, per, embed), tables.dtype),
            vmem((requests, tower_weight.shape[1]), jnp.float32),
            vmem((levels, CORES) + parts_shape[1:], jnp.float32),
            vmem((n_table,) + parts_shape, jnp.float32),
            vmem(tower_weight.shape, tower_weight.dtype),
            vmem(user_proj.shape, user_proj.dtype),
            vmem(cross_weight.shape, cross_weight.dtype),
            vmem((CORES,) + mlp_first.shape, mlp_first.dtype),
            vmem((CORES,) + mlp_second.shape, mlp_second.dtype),
            vmem((CORES,) + bias_row.shape, bias_row.dtype),
            vmem((rows_mine, width), jnp.bfloat16),
            vmem((rows_mine, width), jnp.bfloat16),
            vmem((levels - 1, rows_mine, d_top), jnp.bfloat16),
            vmem((levels - 1, rows_mine, d_top), jnp.bfloat16),
            dma((8,)),
            dma((2, n_cand)),
            dma((2, n_cand)),
            dma((n_table,)),
            dma((n_table,)),
            dma((n_cand, tab_dev)),
            dma((n_cand, tab_dev)),
            dma((n_table, n_cand, tab_dev)),
            dma((n_table, n_cand, tab_dev)),
            dma((levels, n_cand, tab_dev)),
            dma((levels, n_cand, tab_dev)),
            dma((3,)),
            dma((3,)),
            dma((n_table,)),
            dma((n_table,)),
            dma((levels - 1, CUTS, d_top // math.gcd(d_top, 512))),
            dma((levels - 1, CUTS, d_top // math.gcd(d_top, 512))),
        ],
        compiler_params=pltpu.CompilerParams(
            collective_id=0, has_side_effects=True, vmem_limit_bytes=LIMIT
        ),
        name="whole",
    )(
        item_ids,
        user_feats,
        tables.reshape(tab_dev * rows_dev, embed),
        tower_weight,
        tower_bias[None, :],
        user_proj,
        mlp_first,
        mlp_second,
        bias_row,
        cross_weight,
        cross_bias[None, :],
        second_bias[None, :],
        task_weight.T,
        task_bias,
    )


def solution(mesh):
    placed = (
        P("cand", None),
        P(None, "table"),
        P("table"),
        P("table", None),
        P("table", None, "cand"),
        P("table", "cand", None),
        P(),
        P(),
        P(None, "table"),
        P("table"),
        P("table", None),
        P(),
        P(),
        P(),
    )
    return jax.shard_map(
        on_device, mesh=mesh, in_specs=placed, out_specs=P(None, "table", "cand"), check_vma=False
    )
```

```python
import functools
import math

import jax
import jax.numpy as jnp
from jax import lax
from jax.experimental import pallas as pl
from jax.experimental.pallas import tpu as pltpu
from jax.sharding import PartitionSpec as P

MESH = pl.DeviceIdType.MESH
VMEM_SPEC = pl.BlockSpec(memory_space=pltpu.VMEM)
SMEM_SPEC = pl.BlockSpec(memory_space=pltpu.SMEM)
ANY_SPEC = pl.BlockSpec(memory_space=pl.ANY)
CORES = 2
LANES = 128
CUTS = 2
LIMIT = 62 << 20


def push(src, dst, send, recv, axis, peer):
    return pltpu.make_async_remote_copy(
        src_ref=src,
        dst_ref=dst,
        send_sem=send,
        recv_sem=recv,
        device_id={axis: peer},
        device_id_type=MESH,
    )


def widen(src, dst, rows):
    size = math.gcd(rows, 256)

    def body(i, carry):
        at = pl.multiple_of(i * size, size)
        dst[pl.ds(at, size), :] = src[pl.ds(at, size), :].astype(jnp.float32)
        return carry

    lax.fori_loop(0, rows // size, body, 0)


def whole_kernel(
    n,
    n_table,
    cap,
    rows_dev,
    items,
    feats,
    tab,
    tower_w,
    tower_b,
    proj_w,
    first,
    second,
    bias,
    cross_w,
    cross_b,
    second_b,
    task_w,
    task_b,
    out,
    ids_o,
    ids_v,
    ids_s,
    spots,
    columns,
    feats_v,
    feats_f,
    tab_v,
    wide,
    found,
    blocks,
    summed,
    partial,
    parts,
    w_held,
    p_held,
    cross_v,
    first_v,
    second_v,
    biases,
    base,
    crossed,
    sent,
    got,
    load,
    id_send,
    id_recv,
    spot_send,
    spot_recv,
    row_send,
    row_recv,
    mate_send,
    mate_recv,
    level_send,
    level_recv,
    w_send,
    w_recv,
    part_send,
    part_recv,
    top_send,
    top_recv,
):
    me = lax.axis_index("cand")
    place = lax.axis_index("table")
    core = lax.rem(place, CORES)
    level = place // CORES
    levels = n_table // CORES
    mate = place + 1 - 2 * core
    tab_dev, all_requests, cand_dev = items.shape
    group = max(1, LANES // cand_dev)
    steps, lanes = all_requests // group, group * cand_dev
    per = tab_dev * cap
    lines = per // LANES
    embed = wide.shape[1]
    row_all = columns.shape[0]
    rows, width = base.shape
    tables_all = n_table * tab_dev
    tasks, requests, _ = out.shape

    tab_copy = pltpu.make_async_copy(tab, tab_v.at[pl.ds(0, tab.shape[0]), :], load.at[0])
    w_copy = pltpu.make_async_copy(tower_w, w_held, load.at[1])
    p_copy = pltpu.make_async_copy(proj_w, p_held, load.at[2])
    held = [
        pltpu.make_async_copy(src, dst, load.at[5 + i])
        for i, (src, dst) in enumerate(
            ((cross_w, cross_v), (first, first_v.at[0]), (second, second_v.at[0]))
        )
    ]
    tab_copy.start()
    barrier = pltpu.get_barrier_semaphore()
    for d in range(1, n):
        pl.semaphore_signal(
            barrier, inc=1, device_id={"cand": lax.rem(me + d, n)}, device_id_type=MESH
        )
    for d in range(1, n_table):
        pl.semaphore_signal(
            barrier,
            inc=1,
            device_id={"table": lax.rem(place + d, n_table)},
            device_id_type=MESH,
        )

    owners = lax.broadcasted_iota(jnp.int32, (n, lanes), 0)
    sender = lax.broadcasted_iota(jnp.int32, (lanes, 2 * lanes), 0)
    reader = lax.broadcasted_iota(jnp.int32, (lanes, 2 * lanes), 1)
    counting = jnp.where((sender < reader) | (reader >= lanes), 1.0, 0.0).astype(jnp.bfloat16)
    slots = lax.broadcasted_iota(jnp.int32, (cap, lanes), 0).astype(jnp.float32)
    share = steps // n_table
    for t in range(tab_dev):
        joined = jnp.concatenate(
            [items[t, pl.ds(g, steps, stride=group), :] for g in range(group)], axis=1
        )
        owner = joined // rows_dev
        local = joined - owner * rows_dev
        hots = []
        for j in range(steps):
            hots.append(jnp.where(owner[j : j + 1, :] == owners, 1.0, 0.0))
        counts = jnp.dot(
            jnp.concatenate(hots, axis=0).astype(jnp.bfloat16),
            counting,
            preferred_element_type=jnp.float32,
        )
        before = jnp.zeros((n, lanes), jnp.float32)
        total = jnp.zeros((2 * n, cap), jnp.float32)
        for j in range(steps):
            hot = hots[j]
            mine = counts[j * n : (j + 1) * n, :]
            spot = jnp.sum(hot * (mine[:, 0:lanes] + before), axis=0, keepdims=True)
            before = before + mine[:, lanes:]
            spots[place, j // share, t, j % share : j % share + 1, :] = (
                spot + (owner[j : j + 1, :] * cap).astype(jnp.float32)
            )
            row = local[j : j + 1, :]
            low = (row & (LANES - 1)).astype(jnp.float32)
            high = (row // LANES).astype(jnp.float32)
            digits = jnp.concatenate([hot * low, hot * high], axis=0).astype(jnp.bfloat16)
            at = jnp.where(slots == spot, 1.0, 0.0).astype(jnp.bfloat16)
            total = total + lax.dot_general(
                digits, at, (((1,), (1,)), ((), ())), preferred_element_type=jnp.float32
            )
        listed = (total[0:n] + total[n:] * float(LANES)).astype(jnp.int32) + t * rows_dev
        listed = jnp.minimum(jnp.maximum(listed, 0), tab.shape[0] - 1)
        for o in range(n):
            for h in range(cap // LANES):
                line = t * (cap // LANES) + h
                ids_o[o, line : line + 1, :] = listed[o : o + 1, h * LANES : (h + 1) * LANES]
    own_ids = pltpu.make_async_copy(ids_o.at[me], ids_s.at[0], load.at[3])
    own_ids.start()
    pl.semaphore_wait(barrier, n + n_table - 2)

    def across(d):
        bit, peer = 1, 0
        while bit < n:
            mine, other = lax.rem(me // bit, 2), lax.rem(d // bit, 2)
            peer += bit * (mine + other - 2 * mine * other)
            bit *= 2
        return peer

    def id_copy(d):
        peer = across(d)
        return push(ids_o.at[peer], ids_v.at[d], id_send.at[0, d], id_recv.at[0, d], "cand", peer)

    def feat_copy(d):
        peer = across(d)
        return push(feats, feats_v.at[me], id_send.at[1, d], id_recv.at[1, d], "cand", peer)

    def spot_of(d, i):
        return pl.ds(pl.multiple_of(d * per + i * cap, cap), cap)

    def row_copy(d, i):
        peer = across(d)
        to = blocks.at[place, d, pl.ds(i * cap, cap)]
        return push(
            tab_v.at[spot_of(d, i), :], to, row_send.at[d, i], row_recv.at[d, i], "cand", peer
        )

    def mate_copy(p, d, i):
        block = blocks.at[p, d, pl.ds(i * cap, cap)]
        return push(block, block, mate_send.at[p, d, i], mate_recv.at[p, d, i], "table", mate)

    def level_copy(up, d, i):
        block = blocks.at[place, d, pl.ds(i * cap, cap)]
        peer = lax.rem(level + up, levels) * CORES + core
        return push(
            block, block, level_send.at[up, d, i], level_recv.at[up, d, i], "table", peer
        )

    def each(low, high, act):
        def body(d, carry):
            act(d)
            return carry

        lax.fori_loop(low, high, body, 0)

    each(1, n, lambda d: id_copy(d).start())
    spot_copies = [
        push(
            spots.at[place],
            spots.at[place],
            spot_send.at[d],
            spot_recv.at[d],
            "table",
            lax.rem(place + d, n_table),
        )
        for d in range(1, n_table)
    ]
    for copy in spot_copies:
        copy.start()
    each(1, n, lambda d: feat_copy(d).start())
    swaps = [
        push(src, dst, w_send.at[i], w_recv.at[i], "table", mate)
        for i, (src, dst) in enumerate(
            ((first, first_v.at[1]), (second, second_v.at[1]), (bias, biases.at[1]))
        )
    ]
    biases[0] = bias[...]
    feats_v[me] = feats[...]
    tab_copy.wait()
    w_copy.start()
    p_copy.start()
    for copy in held:
        copy.start()
    for copy in swaps:
        copy.start()
    widen(tab_v, wide, tab.shape[0])

    def gather(d, i, into):
        share_of = cap // LANES

        def body(line, carry):
            at = pl.multiple_of(line * LANES, LANES)
            taken = [ids_s[d, i * share_of + line, j] for j in range(LANES)]
            for b in range(0, LANES, 16):
                values = [wide[pl.ds(row, 1), :] for row in taken[b : b + 16]]
                for j, value in enumerate(values):
                    found[pl.ds(at + b + j, 1), :] = value
            into[pl.ds(at, LANES), :] = found[pl.ds(at, LANES), :].astype(jnp.bfloat16)
            return carry

        lax.fori_loop(0, share_of, body, 0)

    def forward(d, i):
        level_starts = [level_copy(up, d, i) for up in range(1, levels)]
        for copy in level_starts:
            copy.start()
        mate_copy(place, d, i).start()

    own_ids.wait()
    for i in range(tab_dev):
        gather(0, i, blocks.at[place, 0, pl.ds(i * cap, cap)])
        forward(0, i)
    each(1, n, lambda d: id_copy(d).wait_recv())
    to_scalar = pltpu.make_async_copy(
        ids_v.at[pl.ds(1, n - 1)], ids_s.at[pl.ds(1, n - 1)], load.at[4]
    )
    to_scalar.start()

    def lender(r):
        return lax.rem(level + r // CORES, levels) * CORES + lax.rem(core + r, CORES)

    for copy in spot_copies:
        copy.wait()
    for lv in range(levels):
        for j in range(share):
            lists = [
                spots[lender(r), lv * CORES + core, i, j : j + 1, :]
                for r in range(n_table)
                for i in range(tab_dev)
            ]
            at = (lv * share + j) * lanes
            columns[at : at + lanes, 0:tables_all] = jnp.concatenate(lists, axis=0).T
    each(1, n, lambda d: feat_copy(d).wait_recv())
    req_dev = feats.shape[0]
    for c in range(n):
        feats_f[c * req_dev : (c + 1) * req_dev, :] = feats_v[c].astype(jnp.float32)

    to_scalar.wait()

    def fill(d):
        for i in range(tab_dev):
            gather(d, i, tab_v.at[spot_of(d, i), :])

    def serve(d):
        for i in range(tab_dev):
            gather(d, i, tab_v.at[spot_of(d, i), :])
            row_copy(d, i).start()

    half = n // 2
    ahead = 2
    each(1, half, serve)
    each(half, min(half + ahead, n), serve)
    for i in range(tab_dev):
        row_copy(1, i).wait_recv()
        forward(1, i)
    each(half + ahead, n - 1, fill)
    for i in range(tab_dev):
        row_copy(2, i).wait_recv()
        forward(2, i)
    fill(n - 1)

    summed[...] = jnp.zeros_like(summed)
    pieces = n // 2
    deep = w_held.shape[0] // pieces
    part_copies = []
    for d in range(1, n_table):
        peer = lax.rem(place + d, n_table)
        part_copies.append(
            push(
                partial.at[:, lax.rem(peer, CORES)],
                parts.at[place],
                part_send.at[d],
                part_recv.at[d],
                "table",
                peer,
            )
        )
    w_copy.wait()
    p_copy.wait()
    chunk = math.gcd(row_all, 256)
    compared = jnp.bfloat16 if cap <= 256 else jnp.float32
    places = lax.broadcasted_iota(jnp.int32, (chunk, cap), 1).astype(jnp.float32).astype(compared)
    one, zero = jnp.ones((), compared), jnp.zeros((), compared)

    def collect(r, d, i, fresh):
        begin = (across(d) * cap).astype(jnp.float32)
        p = lender(r)
        block = blocks[p, d, i * cap : (i + 1) * cap, :]
        t = r * tab_dev + i

        def body(c, carry):
            at = pl.multiple_of(c * chunk, chunk)
            wanted = (columns[pl.ds(at, chunk), t : t + 1] - begin).astype(places.dtype)
            hot = jnp.where(places == wanted, one, zero).astype(jnp.bfloat16)
            to = pl.ds(pl.multiple_of((p * tab_dev + i) * row_all + at, chunk), chunk)
            rows_in = jnp.dot(hot, block, preferred_element_type=jnp.float32)
            wide[to, :] = rows_in if fresh else wide[to, :] + rows_in
            return carry

        lax.fori_loop(0, row_all // chunk, body, 0, unroll=row_all // chunk <= 2)

    def near(d, fresh=False):
        for i in range(tab_dev):
            collect(0, d, i, fresh)
            mate_copy(mate, d, i).wait_recv()
            collect(1, d, i, fresh)

    def from_levels(d):
        for i in range(tab_dev):
            for up in range(1, levels):
                level_copy(up, d, i).wait_recv()
                mate_copy(lender(CORES * (levels - up)), d, i).start()

    def far(d, fresh=False):
        for i in range(tab_dev):
            for up in range(1, levels):
                collect(CORES * up, d, i, fresh)

    def far_mates(d, fresh=False):
        for i in range(tab_dev):
            for up in range(1, levels):
                mate_copy(lender(CORES * up + 1), d, i).wait_recv()
                collect(CORES * up + 1, d, i, fresh)

    def step(s, carry):
        for i in range(tab_dev):

            @pl.when((s > 2) & (s < n))
            def _():
                row_copy(s, i).wait_recv()
                forward(s, i)

            @pl.when((s >= half) & (s + ahead < n))
            def _():
                row_copy(s + ahead, i).start()

        @pl.when(s == 1)
        def _():
            near(0, True)

        @pl.when((s > 1) & (s <= n))
        def _():
            near(s - 1)

        @pl.when((s >= 2) & (s <= n + 1))
        def _():
            from_levels(s - 2)

        @pl.when(s <= pieces)
        def _():
            at = pl.ds(pl.multiple_of((s - 1) * deep, deep), deep)
            summed[...] += jnp.dot(
                feats_f[:, at].astype(jnp.bfloat16), w_held[at, :], preferred_element_type=jnp.float32
            )

        @pl.when(s == pieces)
        def _():
            tower = jnp.maximum(summed[...] + tower_b[...], 0.0).astype(jnp.bfloat16)
            part = jnp.dot(tower, p_held[...], preferred_element_type=jnp.float32)
            quarter = partial.shape[2]
            for q in range(n_table):
                partial[q // CORES, q % CORES] = part[q * quarter : (q + 1) * quarter, :]
            for copy in part_copies:
                copy.start()
            for y in range(levels):
                parts[place, y] = partial[y, core]

        @pl.when(s == 3)
        def _():
            far_mates(0, True)

        @pl.when(s > 3)
        def _():
            far_mates(s - 3)

        @pl.when(s == 2)
        def _():
            far(0, True)

        @pl.when((s > 2) & (s <= n + 1))
        def _():
            far(s - 2)

        return carry

    lax.fori_loop(1, n + 3, step, 0)

    for copy in part_copies + swaps:
        copy.wait()
    for copy in held:
        copy.wait()
    span = max(256, (1 << 18) // rows)
    tile = math.gcd(width, span)
    hidden_tile = math.gcd(first.shape[1], span)
    units, d_top = second.shape
    top_tile = math.gcd(d_top, 512)
    top_copies = []
    for d in range(1, levels + 1):
        at_level = lax.rem(level + d, levels)
        total = parts[0, at_level]
        for q in range(1, n_table):
            total = total + parts[q, at_level]
        proj = total.astype(jnp.bfloat16).astype(jnp.float32)
        cuts = 1 if d == levels else CUTS
        few = rows // cuts
        for cut in range(cuts):
            first_row = cut * few
            mine = slice(first_row, first_row + few)
            for t in range(tables_all):
                lane = slice(t * embed, (t + 1) * embed)
                for r in range(cut * requests // cuts, (cut + 1) * requests // cuts):
                    at = pl.multiple_of(t * row_all + at_level * rows + r * cand_dev, cand_dev)
                    base[r * cand_dev : (r + 1) * cand_dev, lane] = (
                        wide[pl.ds(at, cand_dev), :] + proj[r : r + 1, lane]
                    ).astype(jnp.bfloat16)

            def cross(j, carry):
                at = pl.ds(pl.multiple_of(j * tile, tile), tile)
                product = jnp.dot(base[mine, :], cross_v[:, at], preferred_element_type=jnp.float32)
                broad = base[mine, at].astype(jnp.float32)
                crossed[mine, at] = (broad * (product + cross_b[:, at]) + broad).astype(
                    jnp.bfloat16
                )
                return carry

            lax.fori_loop(0, width // tile, cross, 0)
            for i in range(CORES):

                def layer(j, carry):
                    at = pl.ds(pl.multiple_of(j * hidden_tile, hidden_tile), hidden_tile)
                    hidden = jnp.dot(
                        crossed[mine, :], first_v[i, :, at], preferred_element_type=jnp.float32
                    )
                    hidden = jnp.maximum(hidden + biases[i, :, at], 0.0)
                    start = i * rows + first_row
                    w_held[start : start + few, at] = hidden.astype(jnp.bfloat16)
                    return carry

                lax.fori_loop(0, units // hidden_tile, layer, 0)
            for c in range(d_top // top_tile):
                at = slice(c * top_tile, (c + 1) * top_tile)
                term = jnp.dot(
                    w_held[mine, 0:units], second_v[0, :, at], preferred_element_type=jnp.float32
                )
                for i in range(1, CORES):
                    term += jnp.dot(
                        w_held[i * rows + first_row : i * rows + first_row + few, 0:units],
                        second_v[i, :, at],
                        preferred_element_type=jnp.float32,
                    )
                if d == levels:
                    for h in range(top_tile // embed):
                        to = (c * (top_tile // embed) + h) * rows
                        wide[to : to + rows, :] = term[:, h * embed : (h + 1) * embed]
                    continue
                sent[d - 1, mine, at] = term.astype(jnp.bfloat16)
                top_copies.append(
                    push(
                        sent.at[d - 1, mine, at],
                        got.at[d - 1, mine, at],
                        top_send.at[d - 1, cut, c],
                        top_recv.at[d - 1, cut, c],
                        "table",
                        at_level * CORES + core,
                    )
                )
                top_copies[-1].start()

    def drain(d):
        id_copy(d).wait_send()
        feat_copy(d).wait_send()
        for i in range(tab_dev):
            row_copy(d, i).wait_send()

    def drain_blocks(d):
        for i in range(tab_dev):
            for lv in range(levels):
                mate_copy(lv * CORES + core, d, i).wait_send()
            for up in range(1, levels):
                level_copy(up, d, i).wait_send()

    each(1, n, drain)
    each(0, n, drain_blocks)
    for copy in top_copies:
        copy.wait()
    for c in range(d_top // embed):
        at = slice(c * embed, (c + 1) * embed)
        total = wide[c * rows : (c + 1) * rows, :] + second_b[:, at]
        for d in range(levels - 1):
            total = total + got[d, :, at].astype(jnp.float32)
        crossed[:, at] = jnp.maximum(total, 0.0).astype(jnp.bfloat16)
    for r in range(requests):
        scores = lax.dot_general(
            task_w[...],
            crossed[r * cand_dev : (r + 1) * cand_dev, :],
            (((1,), (1,)), ((), ())),
            preferred_element_type=jnp.float32,
        )
        for k in range(tasks):
            out[k, r : r + 1, :] = scores[k : k + 1, :] + task_b[k]


def on_device(
    user_feats,
    tower_weight,
    tower_bias,
    user_proj,
    item_ids,
    tables,
    cross_weight,
    cross_bias,
    mlp_first,
    first_bias,
    mlp_second,
    second_bias,
    task_weight,
    task_bias,
):
    n_cand = lax.axis_size("cand")
    n_table = lax.axis_size("table")
    tab_dev, requests, cand_dev = item_ids.shape
    rows_dev = tables.shape[1]
    embed = tables.shape[2]
    req_dev, user_width = user_feats.shape
    cap = 2 * req_dev * cand_dev
    row_total = requests * cand_dev
    group = max(1, LANES // cand_dev)
    steps, lanes = requests // group, group * cand_dev
    per = tab_dev * cap
    lines = per // LANES
    levels = n_table // CORES
    bias_row = first_bias[None, :]
    quarter = requests // n_table
    rows_mine = row_total // n_table
    width = n_table * tab_dev * embed
    parts_shape = (levels, quarter, user_proj.shape[1])
    vmem = pltpu.VMEM
    dma = pltpu.SemaphoreType.DMA
    tasks = task_weight.shape[1]
    d_top = mlp_second.shape[1]
    held_rows = max(tab_dev * rows_dev, n_cand * per)
    wide_rows = max(
        tab_dev * rows_dev, n_table * tab_dev * levels * rows_mine, d_top // embed * rows_mine
    )
    return pl.pallas_call(
        functools.partial(whole_kernel, n_cand, n_table, cap, rows_dev),
        out_shape=jax.ShapeDtypeStruct((tasks, quarter, cand_dev), jnp.float32),
        in_specs=[
            VMEM_SPEC,
            VMEM_SPEC,
            ANY_SPEC,
            ANY_SPEC,
            VMEM_SPEC,
            ANY_SPEC,
            ANY_SPEC,
            ANY_SPEC,
            VMEM_SPEC,
            ANY_SPEC,
            VMEM_SPEC,
            VMEM_SPEC,
            VMEM_SPEC,
            SMEM_SPEC,
        ],
        out_specs=VMEM_SPEC,
        scratch_shapes=[
            vmem((n_cand, lines, LANES), jnp.int32),
            vmem((n_cand, lines, LANES), jnp.int32),
            pltpu.SMEM((n_cand, lines, LANES), jnp.int32),
            vmem((n_table, n_table, tab_dev, steps // n_table, lanes), jnp.float32),
            vmem((levels * rows_mine, LANES), jnp.float32),
            vmem((n_cand, req_dev, user_width), user_feats.dtype),
            vmem((requests, user_width), jnp.float32),
            vmem((held_rows, embed), tables.dtype),
            vmem((wide_rows, embed), jnp.float32),
            vmem((per, embed), jnp.float32),
            vmem((n_table, n_cand, per, embed), tables.dtype),
            vmem((requests, tower_weight.shape[1]), jnp.float32),
            vmem((levels, CORES) + parts_shape[1:], jnp.float32),
            vmem((n_table,) + parts_shape, jnp.float32),
            vmem(tower_weight.shape, tower_weight.dtype),
            vmem(user_proj.shape, user_proj.dtype),
            vmem(cross_weight.shape, cross_weight.dtype),
            vmem((CORES,) + mlp_first.shape, mlp_first.dtype),
            vmem((CORES,) + mlp_second.shape, mlp_second.dtype),
            vmem((CORES,) + bias_row.shape, bias_row.dtype),
            vmem((rows_mine, width), jnp.bfloat16),
            vmem((rows_mine, width), jnp.bfloat16),
            vmem((levels - 1, rows_mine, d_top), jnp.bfloat16),
            vmem((levels - 1, rows_mine, d_top), jnp.bfloat16),
            dma((8,)),
            dma((2, n_cand)),
            dma((2, n_cand)),
            dma((n_table,)),
            dma((n_table,)),
            dma((n_cand, tab_dev)),
            dma((n_cand, tab_dev)),
            dma((n_table, n_cand, tab_dev)),
            dma((n_table, n_cand, tab_dev)),
            dma((levels, n_cand, tab_dev)),
            dma((levels, n_cand, tab_dev)),
            dma((3,)),
            dma((3,)),
            dma((n_table,)),
            dma((n_table,)),
            dma((levels - 1, CUTS, d_top // math.gcd(d_top, 512))),
            dma((levels - 1, CUTS, d_top // math.gcd(d_top, 512))),
        ],
        compiler_params=pltpu.CompilerParams(
            collective_id=0, has_side_effects=True, vmem_limit_bytes=LIMIT
        ),
        name="whole",
    )(
        item_ids,
        user_feats,
        tables.reshape(tab_dev * rows_dev, embed),
        tower_weight,
        tower_bias[None, :],
        user_proj,
        mlp_first,
        mlp_second,
        bias_row,
        cross_weight,
        cross_bias[None, :],
        second_bias[None, :],
        task_weight.T,
        task_bias,
    )


def solution(mesh):
    placed = (
        P("cand", None),
        P(None, "table"),
        P("table"),
        P("table", None),
        P("table", None, "cand"),
        P("table", "cand", None),
        P(),
        P(),
        P(None, "table"),
        P("table"),
        P("table", None),
        P(),
        P(),
        P(),
    )
    return jax.shard_map(
        on_device, mesh=mesh, in_specs=placed, out_specs=P(None, "table", "cand"), check_vma=False
    )
```
